768 devices in a mesh: dp: 64 (over y, x, core), tp: 12 (over z).
Axes of the slice: x: 4, y: 8, z: 12, core: 2. Of those that a mesh axis runs over, the one named last changes fastest.
Arguments:
- hidden: bfloat16 [65536, 6144], P('dp', 'tp'), may hold values from -6 to 6
- norm_gain: float32 [6144], P('tp'), may hold values from 0.1 to 1.9
- kv_weight: bfloat16 [6144, 1536], P('tp'), may hold values from -0.078125 to 0.078125
- owners: int32 [65536, 1], P('dp'), may hold values from 0 to 63; in each aligned block of 1024 rows (0 to 1023, 1024 to 2047, ...) at most 32 rows name the same one
- offsets: int32 [65536], P('dp'), may hold values from 0 to 4095
Outputs:
- kv_slots: bfloat16 [1536, 131072], P('tp', 'dp')
The draws below stay inside these ranges and needn't reach their ends.
Inputs may be any that keep to these rules, and one draw needn't show every extreme that they name: `owners`: among the 1024 rows of one group no owner is named more than 32 times, a bound that some block reaches.
All inputs are finite; a program needn't handle non-finite values.
Results may differ from the reference program's by a relative error of at most 0.0049.
Values may be sent and summed in bfloat16 or wider, within the bound.
No kernel may reach another device: no remote copies, remote signals or barrier semaphores. Data moves between devices by JAX's collectives and lax.ppermute only.
A program may use at most 64 MiB of HBM per device.

```python
import math
from functools import partial
import jax
import jax.numpy as jnp
import numpy as np
from jax import lax

D_WIN = 6144
KV_HEADS = 6
HEAD = 128
KV_COLS = 1536
ROWS_DEV = 1024
CAP = 32
TOKENS = 65536
SLOTS = 131072
N_DP = 64


def set_ends(values, own_key, smallest, largest):
    index_at = [jax.random.randint(jax.random.fold_in(own_key, axis), (), 0, length) for axis, length in enumerate(values.shape)]
    longest = values.shape.index(max(values.shape))
    beside = index_at[:longest] + [(index_at[longest] + 1) % values.shape[longest]] + index_at[longest + 1:]
    return values.at[tuple(index_at)].set(smallest).at[tuple(beside)].set(largest)


def levels(key, extent, pieces, least, top_value):
    factor_of, own = 1.0, jax.random.fold_in(key, 6)
    for dim, shards_of in pieces:
        steps = jnp.exp(jax.random.uniform(jax.random.fold_in(own, dim), (shards_of,), jnp.float32, least / len(pieces), top_value / len(pieces)))
        factor_of = factor_of * jnp.repeat(steps, extent[dim] // shards_of).reshape([-1 if axis == dim else 1 for axis in range(len(extent))])
    return factor_of


def shared_out(stream_key, own, number, rows, count, top, reach, skew):
    order = jax.random.permutation(stream_key, count)
    crowded, usual = portions_of(count, rows * top, reach, skew, True), portions_of(count, rows * top, reach, skew, False)
    places = jnp.arange(count)

    def named(sizes, turn):
        used = int((sizes > 0).sum())
        fixed = max(1, used // 4)
        passed = fixed + (places - fixed + turn * (used - fixed)) % max(1, count - fixed)
        return jnp.zeros((count,), jnp.int32).at[order[jnp.where(places < fixed, places, passed)]].set(jnp.asarray(sizes, jnp.int32))

    sizes = jnp.where(number % 4 == 0, named(crowded, number // 4), named(usual, number - number // 4 - 1))
    mixed = jax.random.permutation(jax.random.fold_in(own, 3), count)
    source_of, receiver = mixed[0:count // 2 * 2:2], mixed[1:count // 2 * 2:2]
    room = jnp.minimum(sizes[source_of] - 1, reach - sizes[receiver]) // 2
    room = jnp.where((source_of == order[0]) | (receiver == order[0]) | (sizes[receiver] == 0), 0, jnp.maximum(room, 0))
    passed = jax.random.randint(jax.random.fold_in(own, 4), (count // 2,), 0, 1 << 20) % (room + 1)
    sizes = sizes.at[source_of].add(-passed).at[receiver].add(passed)
    labels = jnp.searchsorted(jnp.cumsum(sizes), jnp.arange(rows * top), side="right").astype(jnp.int32)
    table = labels.reshape(top, rows).T
    table = table[jax.random.permutation(jax.random.fold_in(own, 1), rows)]
    turn = jax.random.randint(jax.random.fold_in(own, 2), (rows, 1), 0, top)
    return jnp.take_along_axis(table, (jnp.arange(top)[None, :] + turn) % top, axis=1)


def portions_of(count, total, reach, skew, full):
    weights = [(1 << 20) // math.isqrt(standing ** skew) + 1 for standing in range(1, count + 1)]
    largest = reach if full else min(reach, max(-(-total // count), total * weights[0] // sum(weights)))
    least = 1 if total - largest >= count - 1 else 0
    given, surplus = [largest] + [least] * (count - 1), total - largest - least * (count - 1)
    while surplus > 0:
        movable = [i for i in range(1, count) if given[i] < largest] or [i for i in range(1, count) if given[i] < reach]
        mass, left = sum([weights[i] for i in movable]), surplus
        for i in movable:
            more = min(reach - given[i], max(1, left * weights[i] // mass), surplus)
            given[i] = given[i] + more
            surplus = surplus - more
    return np.array(given)


def noise(key, extent, spread, bound, pieces=(), kind=jnp.bfloat16):
    values = spread * jax.random.normal(key, extent, jnp.float32)
    if pieces:
        values = values * levels(key, extent, pieces, -0.22, 0.18)
    return jnp.clip(values, -bound, bound).astype(kind)


def setup_inputs(seed: int = 0) -> dict:
    splits = jax.random.split(jax.random.key(seed), 6)
    hidden = noise(splits[0], (TOKENS, D_WIN), 1.0, 6.0, ((0, 64), (1, 12)))
    norm_gain = jnp.clip(1.0 + 0.18 * jax.random.normal(splits[1], (D_WIN,), jnp.float32), 0.1, 1.9)
    kv_weight = noise(splits[2], (D_WIN, KV_COLS), D_WIN ** -0.5, 0.078125, ((0, 12),))
    owners_keys = jax.random.split(jax.random.fold_in(splits[3], 1), TOKENS // ROWS_DEV)
    owners_turns = jax.random.permutation(jax.random.fold_in(splits[3], 3), TOKENS // ROWS_DEV)
    owners = jax.vmap(lambda own, number: shared_out(jax.random.fold_in(splits[3], 2), own, number, ROWS_DEV, N_DP, 1, CAP, 2))(owners_keys, owners_turns).reshape((TOKENS, 1))
    offsets = set_ends(jax.random.randint(splits[4], (TOKENS,), 0, 4096), jax.random.fold_in(splits[4], 1), 0, 4095).astype(jnp.int32)
    return dict(hidden=hidden, norm_gain=norm_gain, kv_weight=kv_weight, owners=owners, offsets=offsets)


EPSILON = 1e-05
ROPE_BASE = 500000.0

def rotate_keys(projected, positions, first_block):
    col_count, row_count = projected.shape
    half_dim = HEAD // 2
    block_count = col_count // HEAD
    exponent = jnp.arange(half_dim, dtype=jnp.float32) * (2.0 / HEAD)
    inverse = ROPE_BASE ** (-exponent)
    angles = inverse[:, None] * positions.astype(jnp.float32)[None, :]
    cosine = jnp.cos(angles)
    sine = jnp.sin(angles)
    blocks = projected.reshape(block_count, 2, half_dim, row_count)
    first_half = blocks[:, 0]
    second_half = blocks[:, 1]
    turned = jnp.stack([first_half * cosine - second_half * sine, second_half * cosine + first_half * sine], axis=1)
    is_key = first_block + jnp.arange(block_count, dtype=jnp.int32) < KV_HEADS
    return jnp.where(is_key[:, None, None, None], turned, blocks).reshape(col_count, row_count)

def rank_within(destination, peers):
    onehot = (destination[:, None] == jnp.arange(peers, dtype=jnp.int32)[None, :]).astype(jnp.int32)
    before = jnp.cumsum(onehot, axis=0) - onehot
    return lax.optimization_barrier(jnp.sum(before * onehot, axis=1)).astype(jnp.int32)

def reference(hidden, norm_gain, kv_weight, owners, offsets):
    widened = hidden.astype(jnp.float32)
    total = lax.optimization_barrier(jnp.sum(widened * widened, axis=1))
    normed = (widened * lax.rsqrt(total / D_WIN + EPSILON)[:, None] * norm_gain[None, :]).astype(jnp.bfloat16)
    projected = lax.dot_general(kv_weight, normed, (((0,), (1,)), ((), ())), preferred_element_type=jnp.float32)
    rotated = rotate_keys(projected, offsets, 0).astype(jnp.bfloat16)
    destination = owners[:, 0].reshape(N_DP, ROWS_DEV)
    within = jax.vmap(partial(rank_within, peers=N_DP))(destination)
    source = jnp.arange(N_DP, dtype=jnp.int32)[:, None]
    target = (destination * (N_DP * CAP) + source * CAP + within).reshape(-1).astype(jnp.int32)
    result = jnp.zeros((KV_COLS, SLOTS), jnp.bfloat16)
    return result.at[:, target].set(rotated)
```

```python
import functools

import jax
import jax.numpy as jnp
from jax import lax
from jax.experimental import pallas as pl
from jax.experimental.pallas import tpu as pltpu
from jax.sharding import PartitionSpec as P

D_WIN = 6144
KV_HEADS = 6
HEAD = 128
EPSILON = 1e-05
ROPE_BASE = 500000.0
TAIL = 32
VM = pltpu.VMEM
SM = pltpu.SMEM
HBM = pltpu.HBM
F32 = jnp.float32
BF16 = jnp.bfloat16


def call(kernel, outs, ins, spaces, us, name, scratch=(), limit=12):
    return pl.pallas_call(
        kernel,
        out_shape=outs,
        in_specs=[pl.BlockSpec(memory_space=s) for s in spaces],
        out_specs=jax.tree.map(lambda _: pl.BlockSpec(memory_space=VM), outs),
        scratch_shapes=list(scratch),
        cost_estimate=pl.CostEstimate(flops=int(us * 5e8), bytes_accessed=int(us * 2e6), transcendentals=0),
        compiler_params=pltpu.CompilerParams(vmem_limit_bytes=limit << 20),
        name=name,
    )(*ins)


def split3(x):
    a = x.astype(BF16).astype(F32)
    b = (x - a).astype(BF16).astype(F32)
    return a, b, x - a - b


def put_tail(o_ref, x):
    pad = jnp.zeros_like(x)
    o_ref[o_ref.shape[0] - TAIL :, :] = jnp.concatenate([*split3(x), pad], axis=0).astype(BF16)


def get_tail(ref):
    t = ref[ref.shape[0] - TAIL :, :].astype(F32)
    n = TAIL // 4
    return t[:n] + t[n : 2 * n] + t[2 * n : 3 * n]


def block_of(w_ref, z, shift, n):
    c = lax.rem(z + shift, n)
    return w_ref[:, pl.ds(pl.multiple_of(c * HEAD, HEAD), HEAD)]


def dot(hi, lo, w):
    return jnp.dot(hi, w, preferred_element_type=F32) + jnp.dot(lo, w, preferred_element_type=F32)


def prep_kernel(row0, shift, n, z_ref, h_ref, g_ref, w_ref, hi_ref, lo_ref, sq_ref, o_ref, h_v, g_v, w_v, sems):
    half = h_v.shape[0]
    c = lax.rem(z_ref[0] + shift, n)
    copies = [
        pltpu.make_async_copy(h_ref.at[pl.ds(row0, half), :], h_v, sems.at[0]),
        pltpu.make_async_copy(g_ref, g_v, sems.at[1]),
        pltpu.make_async_copy(w_ref.at[:, pl.ds(pl.multiple_of(c * HEAD, HEAD), HEAD)], w_v, sems.at[2]),
    ]
    for copy in copies:
        copy.start()
    for copy in copies:
        copy.wait()
    h = h_v[...].astype(F32)
    x = h * g_v[...]
    hi = x.astype(BF16)
    lo = (x - hi.astype(F32)).astype(BF16)
    hi_ref[...] = hi
    lo_ref[...] = lo
    o_ref[:half, :] = dot(hi, lo, w_v[...]).astype(BF16)
    eye = lax.broadcasted_iota(jnp.int32, (HEAD, HEAD), 0) == lax.broadcasted_iota(jnp.int32, (HEAD, HEAD), 1)
    col = jnp.sum(h * h, axis=1, keepdims=True)
    rows = [
        jnp.sum(jnp.where(eye, col[i * HEAD : (i + 1) * HEAD, :], 0.0), axis=0, keepdims=True)
        for i in range(half // HEAD)
    ]
    none = jnp.zeros((TAIL // 4 - len(rows), HEAD), F32)
    sq = jnp.concatenate([*rows, none] if row0 == 0 else [none, *rows], axis=0)
    sq_ref[...] = sq
    put_tail(o_ref, sq)


def term_kernel(shifts, n, z_ref, hia_ref, loa_ref, hib_ref, lob_ref, w_ref, *outs):
    half = hia_ref.shape[0]
    for shift, o_ref in zip(shifts, outs):
        w = block_of(w_ref, z_ref[0], shift, n)
        o_ref[:half, :] = dot(hia_ref[...], loa_ref[...], w)
        o_ref[half:, :] = dot(hib_ref[...], lob_ref[...], w)


def add_kernel(lead, t_ref, sqa_ref, sqb_ref, in_ref, o_ref):
    rows = t_ref.shape[0]
    for start, size in ((0, rows // 2), (rows // 2, rows // 2)):
        at = slice(start, start + size)
        t = t_ref[at, :]
        if lead is None:
            t = t + in_ref[at, :].astype(F32)
        elif lead == start:
            t = t + in_ref[:size, :].astype(F32)
        o_ref[at, :] = t.astype(BF16)
    put_tail(o_ref, sqa_ref[...] + sqb_ref[...] + get_tail(in_ref))


def select_kernel(own_ref, sel_ref):
    rows_dev = own_ref.shape[1]
    slots = sel_ref.shape[0]
    capacity = TAIL
    peers = slots // capacity
    own = own_ref[...]
    one = jnp.where(lax.broadcasted_iota(jnp.int32, (peers, rows_dev), 0) == own, 1.0, 0.0)
    oneb = one.astype(BF16)
    width = 256
    before = jnp.zeros((peers, 1), F32)
    upper = jnp.where(
        lax.broadcasted_iota(jnp.int32, (width, width), 0) < lax.broadcasted_iota(jnp.int32, (width, width), 1), 1.0, 0.0
    ).astype(BF16)
    for i in range(rows_dev // width):
        cols = slice(i * width, (i + 1) * width)
        e = one[:, cols]
        seen = jnp.dot(oneb[:, cols], upper, preferred_element_type=F32) + before
        rank = jnp.sum(seen * e, axis=0, keepdims=True)
        before = before + jnp.sum(e, axis=1, keepdims=True)
        slot = own[:, cols] * capacity + rank.astype(jnp.int32)
        at = lax.broadcasted_iota(jnp.int32, (slots, width), 0)
        sel_ref[:, cols] = jnp.where(at == slot, 1.0, 0.0).astype(BF16)


def finish_kernel(t_ref, sqa_ref, sqb_ref, up_ref, down_ref, cos_ref, sin_ref, sel_ref, o_ref, rot_ref):
    total = sqa_ref[...] + sqb_ref[...] + get_tail(up_ref) + get_tail(down_ref)
    scale = lax.rsqrt(total / D_WIN + EPSILON)
    eye = lax.broadcasted_iota(jnp.int32, (HEAD, HEAD), 0) == lax.broadcasted_iota(jnp.int32, (HEAD, HEAD), 1)
    for i in range(t_ref.shape[0] // HEAD):
        at = slice(i * HEAD, (i + 1) * HEAD)
        col = jnp.sum(jnp.where(eye, scale[i : i + 1, :], 0.0), axis=1, keepdims=True)
        v = (t_ref[at, :] + up_ref[at, :].astype(F32) + down_ref[at, :].astype(F32)) * col
        turned = v * cos_ref[at, :] + pltpu.roll(v, HEAD // 2, 1) * sin_ref[at, :]
        rot_ref[at, :] = turned.astype(BF16)
    o_ref[...] = jnp.dot(sel_ref[...], rot_ref[...], preferred_element_type=F32).astype(BF16)


def per_device(hidden, norm_gain, kv_weight, owners, offsets):
    tp = lax.axis_size("tp")
    peers = lax.axis_size("dp")
    rows_dev, feats = hidden.shape
    capacity = 2 * rows_dev // peers
    slots = peers * capacity
    share = kv_weight.shape[1] // tp
    half = rows_dev // 2
    depth = tp // 2
    z = lax.axis_index("tp").astype(jnp.int32)
    zs = z.reshape(1)
    bf = functools.partial(jax.ShapeDtypeStruct, dtype=BF16)
    fl = functools.partial(jax.ShapeDtypeStruct, dtype=F32)

    def up(a):
        return lax.ppermute(a, "tp", [(i, (i + 1) % tp) for i in range(tp)])

    def down(a):
        return lax.ppermute(a, "tp", [(i, (i - 1) % tp) for i in range(tp)])

    gain = norm_gain.reshape(1, feats)
    halves = []
    for k in (0, 1):
        halves.append(
            call(
                functools.partial(prep_kernel, k * half, depth, tp),
                (bf((half, feats)), bf((half, feats)), fl((TAIL // 4, HEAD)), bf((half + TAIL, share))),
                (zs, hidden, gain, kv_weight),
                (SM, HBM, HBM, HBM),
                2,
                "prep",
                scratch=(VM((half, feats), BF16), VM((1, feats), F32), VM((feats, share), BF16), pltpu.SemaphoreType.DMA((3,))),
            )
        )
    (hia, loa, sqa, ua), (hib, lob, sqb, db) = halves
    got_up, got_down = up(ua), down(db)

    sel = call(select_kernel, bf((slots, rows_dev)), (owners.reshape(1, rows_dev),), (VM,), 2, "select")
    exponent = jnp.arange(HEAD // 2, dtype=F32) * (2.0 / HEAD)
    inverse = ROPE_BASE ** (-exponent)
    angles = offsets.astype(F32)[:, None] * jnp.concatenate([inverse, inverse])[None, :]
    is_key = z * (share // HEAD) < KV_HEADS
    cosine = jnp.where(is_key, jnp.cos(angles), 1.0)
    sign = jnp.where(jnp.arange(HEAD) < HEAD // 2, -1.0, 1.0)[None, :]
    sine = jnp.where(is_key, jnp.sin(angles) * sign, 0.0)

    def terms(*shifts):
        return call(
            functools.partial(term_kernel, shifts, tp),
            tuple(fl((rows_dev, share)) for _ in shifts),
            (zs, hia, loa, hib, lob, kv_weight),
            (SM,) + (VM,) * 5,
            0.8 * len(shifts),
            "term",
        )

    def add(lead, t, message):
        return call(
            functools.partial(add_kernel, lead),
            bf((rows_dev + TAIL, share)),
            (t, sqa, sqb, message),
            (VM,) * 4,
            0.2,
            "add",
        )

    for s in range(2, depth + 1):
        tu, td = terms(depth + 1 - s, tp - (depth + 1 - s))
        lead_up, lead_down = (0, half) if s == 2 else (None, None)
        got_up = up(add(lead_up, tu, got_up))
        got_down = down(add(lead_down, td, got_down))
    (own,) = terms(0)
    out = call(
        finish_kernel,
        bf((slots, share)),
        (own, sqa, sqb, got_up, got_down, cosine, sine, sel),
        (VM,) * 8,
        3,
        "finish",
        scratch=(VM((rows_dev, share), BF16),),
    )
    received = lax.all_to_all(out.reshape(peers, capacity, share), "dp", split_axis=0, concat_axis=0, tiled=True)
    return received.reshape(slots, share).T


def solution(mesh):
    in_specs = (P("dp", "tp"), P("tp"), P("tp", None), P("dp", None), P("dp"))
    return jax.shard_map(per_device, mesh=mesh, in_specs=in_specs, out_specs=P("tp", "dp"), check_vma=False)
```

```python
import functools

import jax
import jax.numpy as jnp
import numpy as np
from jax import lax
from jax.experimental import pallas as pl
from jax.experimental.pallas import tpu as pltpu
from jax.sharding import PartitionSpec as P

D_WIN = 6144
KV_HEADS = 6
HEAD = 128
EPSILON = 1e-05
ROPE_BASE = 500000.0
PREP_LIMIT = 12
TAIL = 32
VM = pltpu.VMEM
SM = pltpu.SMEM
HBM = pltpu.HBM
F32 = jnp.float32
BF16 = jnp.bfloat16
FREQ = np.tile(ROPE_BASE ** (-np.arange(HEAD // 2) * (2.0 / HEAD)), 2).astype(np.float32)


def call(kernel, outs, ins, spaces, us, name, scratch=(), limit=12):
    return pl.pallas_call(
        kernel,
        out_shape=outs,
        in_specs=[pl.BlockSpec(memory_space=s) for s in spaces],
        out_specs=jax.tree.map(lambda _: pl.BlockSpec(memory_space=VM), outs),
        scratch_shapes=list(scratch),
        cost_estimate=pl.CostEstimate(flops=int(us * 5e8), bytes_accessed=int(us * 2e6), transcendentals=0),
        compiler_params=pltpu.CompilerParams(vmem_limit_bytes=limit << 20),
        name=name,
    )(*ins)


def split3(x):
    a = x.astype(BF16).astype(F32)
    b = (x - a).astype(BF16).astype(F32)
    return a, b, x - a - b


def put_tail(o_ref, x):
    pad = jnp.zeros_like(x)
    o_ref[o_ref.shape[0] - TAIL :, :] = jnp.concatenate([*split3(x), pad], axis=0).astype(BF16)


def get_tail(ref):
    t = ref[ref.shape[0] - TAIL :, :].astype(F32)
    n = TAIL // 4
    return t[:n] + t[n : 2 * n] + t[2 * n : 3 * n]


def block_of(w_ref, z, shift, n):
    c = lax.rem(z + shift, n)
    return w_ref[:, pl.ds(pl.multiple_of(c * HEAD, HEAD), HEAD)]


def dot(hi, lo, w):
    return jnp.dot(hi, w, preferred_element_type=F32) + jnp.dot(lo, w, preferred_element_type=F32)


def prep_kernel(row0, shift, n, z_ref, h_ref, g_ref, w_ref, hi_ref, lo_ref, sq_ref, o_ref, h_v, g_v, w_v, sems):
    half = h_v.shape[0]
    c = lax.rem(z_ref[0] + shift, n)
    copies = [
        pltpu.make_async_copy(h_ref.at[pl.ds(row0, half), :], h_v, sems.at[0]),
        pltpu.make_async_copy(g_ref, g_v, sems.at[1]),
        pltpu.make_async_copy(w_ref.at[:, pl.ds(pl.multiple_of(c * HEAD, HEAD), HEAD)], w_v, sems.at[2]),
    ]
    for copy in copies:
        copy.start()
    for copy in copies:
        copy.wait()
    h = h_v[...].astype(F32)
    x = h * g_v[...]
    hi = x.astype(BF16)
    lo = (x - hi.astype(F32)).astype(BF16)
    hi_ref[...] = hi
    lo_ref[...] = lo
    o_ref[:half, :] = dot(hi, lo, w_v[...]).astype(BF16)
    eye = lax.broadcasted_iota(jnp.int32, (HEAD, HEAD), 0) == lax.broadcasted_iota(jnp.int32, (HEAD, HEAD), 1)
    col = jnp.sum(h * h, axis=1, keepdims=True)
    rows = [
        jnp.sum(jnp.where(eye, col[i * HEAD : (i + 1) * HEAD, :], 0.0), axis=0, keepdims=True)
        for i in range(half // HEAD)
    ]
    none = jnp.zeros((TAIL // 4 - len(rows), HEAD), F32)
    sq = jnp.concatenate([*rows, none] if row0 == 0 else [none, *rows], axis=0)
    sq_ref[...] = sq
    put_tail(o_ref, sq)


def term_kernel(shifts, n, extra, n_extra, z_ref, hia_ref, loa_ref, hib_ref, lob_ref, w_ref, *refs):
    half = hia_ref.shape[0]
    ins, outs = refs[:n_extra], refs[n_extra:]
    w = jnp.concatenate([block_of(w_ref, z_ref[0], shift, n) for shift in shifts], axis=1)
    for at, hi_ref, lo_ref in ((slice(0, half), hia_ref, loa_ref), (slice(half, 2 * half), hib_ref, lob_ref)):
        t = dot(hi_ref[...], lo_ref[...], w)
        for i in range(len(shifts)):
            outs[i][at, :] = t[:, i * HEAD : (i + 1) * HEAD]
    if extra is not None:
        extra(z_ref, *ins, *outs[len(shifts) :])


def add_kernel(lead, t_ref, sqa_ref, sqb_ref, in_ref, o_ref):
    rows = t_ref.shape[0]
    for start, size in ((0, rows // 2), (rows // 2, rows // 2)):
        at = slice(start, start + size)
        t = t_ref[at, :]
        if lead is None:
            t = t + in_ref[at, :].astype(F32)
        elif lead == start:
            t = t + in_ref[:size, :].astype(F32)
        o_ref[at, :] = t.astype(BF16)
    put_tail(o_ref, sqa_ref[...] + sqb_ref[...] + get_tail(in_ref))


def select_piece(row0, z_ref, own_ref, sel_ref):
    slots, rows = sel_ref.shape
    capacity = TAIL
    peers = slots // capacity
    own = own_ref[...]
    one = jnp.where(lax.broadcasted_iota(jnp.int32, (peers, own.shape[1]), 0) == own, 1.0, 0.0)
    width = 256
    before = jnp.sum(one[:, :row0], axis=1, keepdims=True) if row0 else jnp.zeros((peers, 1), F32)
    upper = jnp.where(
        lax.broadcasted_iota(jnp.int32, (width, width), 0) < lax.broadcasted_iota(jnp.int32, (width, width), 1), 1.0, 0.0
    ).astype(BF16)
    for i in range(rows // width):
        cols = slice(row0 + i * width, row0 + (i + 1) * width)
        e = one[:, cols]
        seen = jnp.dot(e.astype(BF16), upper, preferred_element_type=F32) + before
        rank = jnp.sum(seen * e, axis=0, keepdims=True)
        before = before + jnp.sum(e, axis=1, keepdims=True)
        slot = own[:, cols] * capacity + rank.astype(jnp.int32)
        at = lax.broadcasted_iota(jnp.int32, (slots, width), 0)
        sel_ref[:, i * width : (i + 1) * width] = jnp.where(at == slot, 1.0, 0.0).astype(BF16)


def identity():
    return lax.broadcasted_iota(jnp.int32, (HEAD, HEAD), 0) == lax.broadcasted_iota(jnp.int32, (HEAD, HEAD), 1)


def table_piece(row0, per_device, z_ref, pos_ref, freq_ref, cos_ref, sin_ref):
    rows = cos_ref.shape[0]
    is_key = z_ref[0] * per_device < KV_HEADS

    @pl.when(is_key)
    def _():
        eye = identity()
        sign = jnp.where(lax.broadcasted_iota(jnp.int32, (1, HEAD), 1) < HEAD // 2, -1.0, 1.0)
        for i in range(rows // HEAD):
            pos = pos_ref[:, row0 + i * HEAD : row0 + (i + 1) * HEAD].astype(F32)
            col = jnp.sum(jnp.where(eye, pos, 0.0), axis=1, keepdims=True)
            angle = col * freq_ref[...]
            at = slice(i * HEAD, (i + 1) * HEAD)
            cos_ref[at, :] = jnp.cos(angle)
            sin_ref[at, :] = jnp.sin(angle) * sign

    @pl.when(jnp.logical_not(is_key))
    def _():
        cos_ref[...] = jnp.ones_like(cos_ref)
        sin_ref[...] = jnp.zeros_like(sin_ref)


def finish_kernel(t_ref, sqa_ref, sqb_ref, up_ref, down_ref, cosa_ref, sina_ref, cosb_ref, sinb_ref, sela_ref, selb_ref, o_ref, rot_ref):
    total = sqa_ref[...] + sqb_ref[...] + get_tail(up_ref) + get_tail(down_ref)
    scale = lax.rsqrt(total / D_WIN + EPSILON)
    eye = identity()
    half = cosa_ref.shape[0]
    out = None
    for row0, cos_ref, sin_ref, sel_ref in ((0, cosa_ref, sina_ref, sela_ref), (half, cosb_ref, sinb_ref, selb_ref)):
        for i in range(half // HEAD):
            at = slice(row0 + i * HEAD, row0 + (i + 1) * HEAD)
            here = slice(i * HEAD, (i + 1) * HEAD)
            r = row0 // HEAD + i
            col = jnp.sum(jnp.where(eye, scale[r : r + 1, :], 0.0), axis=1, keepdims=True)
            v = (t_ref[at, :] + up_ref[at, :].astype(F32) + down_ref[at, :].astype(F32)) * col
            turned = v * cos_ref[here, :] + pltpu.roll(v, HEAD // 2, 1) * sin_ref[here, :]
            rot_ref[at, :] = turned.astype(BF16)
        part = jnp.dot(sel_ref[...], rot_ref[row0 : row0 + half, :], preferred_element_type=F32)
        out = part if out is None else out + part
    o_ref[...] = out.astype(BF16)


def per_device(hidden, norm_gain, kv_weight, owners, offsets):
    tp = lax.axis_size("tp")
    peers = lax.axis_size("dp")
    rows_dev, feats = hidden.shape
    capacity = 2 * rows_dev // peers
    slots = peers * capacity
    share = kv_weight.shape[1] // tp
    half = rows_dev // 2
    depth = tp // 2
    z = lax.axis_index("tp").astype(jnp.int32)
    zs = z.reshape(1)
    bf = functools.partial(jax.ShapeDtypeStruct, dtype=BF16)
    fl = functools.partial(jax.ShapeDtypeStruct, dtype=F32)

    def up(a):
        return lax.ppermute(a, "tp", [(i, (i + 1) % tp) for i in range(tp)])

    def down(a):
        return lax.ppermute(a, "tp", [(i, (i - 1) % tp) for i in range(tp)])

    gain = norm_gain.reshape(1, feats)
    stay = functools.partial(pltpu.with_memory_space_constraint, memory_space=HBM)
    hidden_h, gain_h, weight_h = stay(hidden), stay(gain), stay(kv_weight)
    halves = []
    for k in (0, 1):
        halves.append(
            call(
                functools.partial(prep_kernel, k * half, depth, tp),
                (bf((half, feats)), bf((half, feats)), fl((TAIL // 4, HEAD)), bf((half + TAIL, share))),
                (zs, hidden_h, gain_h, weight_h),
                (SM, HBM, HBM, HBM),
                2,
                "prep",
                limit=PREP_LIMIT,
                scratch=(VM((half, feats), BF16), VM((1, feats), F32), VM((feats, share), BF16), pltpu.SemaphoreType.DMA((3,))),
            )
        )
    (hia, loa, sqa, ua), (hib, lob, sqb, db) = halves
    got_up, got_down = up(ua), down(db)

    own = owners.reshape(1, rows_dev)
    pos = offsets.reshape(1, rows_dev)
    freq = jnp.asarray(FREQ).reshape(1, HEAD)

    def terms(shifts, extra=None, ins=(), extra_outs=(), us=1.0):
        outs = tuple(fl((rows_dev, share)) for _ in shifts) + tuple(extra_outs)
        return call(
            functools.partial(term_kernel, shifts, tp, extra, len(ins)),
            outs,
            (zs, hia, loa, hib, lob, kv_weight) + tuple(ins),
            (SM,) + (VM,) * (5 + len(ins)),
            us,
            "term",
        )

    heads = share // HEAD
    pieces = {
        3: (functools.partial(select_piece, 0), (own,), (bf((slots, half)),)),
        4: (functools.partial(select_piece, half), (own,), (bf((slots, half)),)),
        5: (functools.partial(table_piece, 0, heads), (pos, freq), (fl((half, HEAD)),) * 2),
        6: (functools.partial(table_piece, half, heads), (pos, freq), (fl((half, HEAD)),) * 2),
    }
    extras = []

    def add(lead, t, message):
        return call(
            functools.partial(add_kernel, lead),
            bf((rows_dev + TAIL, share)),
            (t, sqa, sqb, message),
            (VM,) * 4,
            0.2,
            "add",
        )

    for s in range(2, depth + 1):
        tu, td, *more = terms((depth + 1 - s, tp - (depth + 1 - s)), *pieces.get(s, ()))
        extras += more
        lead_up, lead_down = (0, half) if s == 2 else (None, None)
        got_up = up(add(lead_up, tu, got_up))
        got_down = down(add(lead_down, td, got_down))
    (mine,) = terms((0,), us=0.8)
    sela, selb, cosa, sina, cosb, sinb = extras
    out = call(
        finish_kernel,
        bf((slots, share)),
        (mine, sqa, sqb, got_up, got_down, cosa, sina, cosb, sinb, sela, selb),
        (VM,) * 11,
        3,
        "finish",
        scratch=(VM((rows_dev, share), BF16),),
    )
    received = lax.all_to_all(out.reshape(peers, capacity, share), "dp", split_axis=0, concat_axis=0, tiled=True)
    return received.reshape(slots, share).T


def solution(mesh):
    in_specs = (P("dp", "tp"), P("tp"), P("tp", None), P("dp", None), P("dp"))
    return jax.shard_map(per_device, mesh=mesh, in_specs=in_specs, out_specs=P("tp", "dp"), check_vma=False)
```

```python
import functools

import jax
import jax.numpy as jnp
import numpy as np
from jax import lax
from jax.experimental import pallas as pl
from jax.experimental.pallas import tpu as pltpu
from jax.sharding import PartitionSpec as P

D_WIN = 6144
KV_HEADS = 6
HEAD = 128
EPSILON = 1e-05
ROPE_BASE = 500000.0
PREP_LIMIT = 12
TAIL = 32
VM = pltpu.VMEM
SM = pltpu.SMEM
HBM = pltpu.HBM
F32 = jnp.float32
BF16 = jnp.bfloat16
FREQ = np.tile(ROPE_BASE ** (-np.arange(HEAD // 2) * (2.0 / HEAD)), 2).astype(np.float32)


def call(kernel, outs, ins, spaces, us, name, scratch=(), limit=12):
    return pl.pallas_call(
        kernel,
        out_shape=outs,
        in_specs=[pl.BlockSpec(memory_space=s) for s in spaces],
        out_specs=jax.tree.map(lambda _: pl.BlockSpec(memory_space=VM), outs),
        scratch_shapes=list(scratch),
        cost_estimate=pl.CostEstimate(flops=int(us * 5e8), bytes_accessed=int(us * 2e6), transcendentals=0),
        compiler_params=pltpu.CompilerParams(vmem_limit_bytes=limit << 20),
        name=name,
    )(*ins)


def split3(x):
    a = x.astype(BF16).astype(F32)
    b = (x - a).astype(BF16).astype(F32)
    return a, b, x - a - b


def put_tail(o_ref, x):
    pad = jnp.zeros_like(x)
    o_ref[o_ref.shape[0] - TAIL :, :] = jnp.concatenate([*split3(x), pad], axis=0).astype(BF16)


def get_tail(ref):
    t = ref[ref.shape[0] - TAIL :, :].astype(F32)
    n = TAIL // 4
    return t[:n] + t[n : 2 * n] + t[2 * n : 3 * n]


def block_of(w_ref, z, shift, n):
    c = lax.rem(z + shift, n)
    return w_ref[:, pl.ds(pl.multiple_of(c * HEAD, HEAD), HEAD)]


def dot(hi, lo, w):
    return jnp.dot(hi, w, preferred_element_type=F32) + jnp.dot(lo, w, preferred_element_type=F32)


def prep_kernel(shift, n, z_ref, h_ref, g_ref, w_ref, hi_ref, lo_ref, sq_ref, o_ref, h_v, g_v, w_v, sems):
    parts = h_v.shape[0]
    rows = h_v.shape[1]
    c = lax.rem(z_ref[0] + shift, n)
    first = [
        pltpu.make_async_copy(g_ref, g_v, sems.at[parts]),
        pltpu.make_async_copy(w_ref.at[:, pl.ds(pl.multiple_of(c * HEAD, HEAD), HEAD)], w_v, sems.at[parts + 1]),
    ]
    copies = [pltpu.make_async_copy(h_ref.at[pl.ds(p * rows, rows), :], h_v.at[p], sems.at[p]) for p in range(parts)]
    for copy in (copies[0], *first, *copies[1:]):
        copy.start()
    for copy in first:
        copy.wait()
    eye = identity()
    sums = []
    for p in range(parts):
        copies[p].wait()
        at = slice(p * rows, (p + 1) * rows)
        h = h_v[p].astype(F32)
        x = h * g_v[...]
        hi = x.astype(BF16)
        lo = (x - hi.astype(F32)).astype(BF16)
        hi_ref[at, :] = hi
        lo_ref[at, :] = lo
        o_ref[at, :] = dot(hi, lo, w_v[...]).astype(BF16)
        col = jnp.sum(h * h, axis=1, keepdims=True)
        for i in range(rows // HEAD):
            sums.append(jnp.sum(jnp.where(eye, col[i * HEAD : (i + 1) * HEAD, :], 0.0), axis=0, keepdims=True))
    sq = jnp.concatenate(sums, axis=0)
    sq_ref[...] = sq
    put_tail(o_ref, sq)


def term_kernel(shifts, n, extra, n_extra, z_ref, hi_ref, lo_ref, w_ref, *refs):
    ins, outs = refs[:n_extra], refs[n_extra:]
    w = jnp.concatenate([block_of(w_ref, z_ref[0], shift, n) for shift in shifts], axis=1)
    rows = hi_ref.shape[0] // 2
    for at in (slice(0, rows), slice(rows, 2 * rows)):
        t = dot(hi_ref[at, :], lo_ref[at, :], w)
        for i in range(len(shifts)):
            outs[i][at, :] = t[:, i * HEAD : (i + 1) * HEAD]
    if extra is not None:
        extra(z_ref, *ins, *outs[len(shifts) :])


def first_kernel(shift, n, z_ref, hi_ref, lo_ref, w_ref, sq_ref, o_ref):
    w = block_of(w_ref, z_ref[0], shift, n)
    rows = hi_ref.shape[0] // 2
    for at in (slice(0, rows), slice(rows, 2 * rows)):
        o_ref[at, :] = dot(hi_ref[at, :], lo_ref[at, :], w).astype(BF16)
    put_tail(o_ref, sq_ref[...])


def add_kernel(t_ref, sq_ref, in_ref, o_ref):
    rows = t_ref.shape[0]
    o_ref[:rows, :] = (t_ref[...] + in_ref[:rows, :].astype(F32)).astype(BF16)
    put_tail(o_ref, sq_ref[...] + get_tail(in_ref))


def select_piece(row0, z_ref, own_ref, sel_ref):
    slots, rows = sel_ref.shape
    capacity = TAIL
    peers = slots // capacity
    own = own_ref[...]
    one = jnp.where(lax.broadcasted_iota(jnp.int32, (peers, own.shape[1]), 0) == own, 1.0, 0.0)
    width = 256
    before = jnp.sum(one[:, :row0], axis=1, keepdims=True) if row0 else jnp.zeros((peers, 1), F32)
    upper = jnp.where(
        lax.broadcasted_iota(jnp.int32, (width, width), 0) < lax.broadcasted_iota(jnp.int32, (width, width), 1), 1.0, 0.0
    ).astype(BF16)
    for i in range(rows // width):
        cols = slice(row0 + i * width, row0 + (i + 1) * width)
        e = one[:, cols]
        seen = jnp.dot(e.astype(BF16), upper, preferred_element_type=F32) + before
        rank = jnp.sum(seen * e, axis=0, keepdims=True)
        before = before + jnp.sum(e, axis=1, keepdims=True)
        slot = own[:, cols] * capacity + rank.astype(jnp.int32)
        at = lax.broadcasted_iota(jnp.int32, (slots, width), 0)
        sel_ref[:, i * width : (i + 1) * width] = jnp.where(at == slot, 1.0, 0.0).astype(BF16)


def identity():
    return lax.broadcasted_iota(jnp.int32, (HEAD, HEAD), 0) == lax.broadcasted_iota(jnp.int32, (HEAD, HEAD), 1)


def table_piece(row0, per_device, z_ref, pos_ref, freq_ref, cos_ref, sin_ref):
    rows = cos_ref.shape[0]
    is_key = z_ref[0] * per_device < KV_HEADS

    @pl.when(is_key)
    def _():
        eye = identity()
        sign = jnp.where(lax.broadcasted_iota(jnp.int32, (1, HEAD), 1) < HEAD // 2, -1.0, 1.0)
        for i in range(rows // HEAD):
            pos = pos_ref[:, row0 + i * HEAD : row0 + (i + 1) * HEAD].astype(F32)
            col = jnp.sum(jnp.where(eye, pos, 0.0), axis=1, keepdims=True)
            angle = col * freq_ref[...]
            at = slice(i * HEAD, (i + 1) * HEAD)
            cos_ref[at, :] = jnp.cos(angle)
            sin_ref[at, :] = jnp.sin(angle) * sign

    @pl.when(jnp.logical_not(is_key))
    def _():
        cos_ref[...] = jnp.ones_like(cos_ref)
        sin_ref[...] = jnp.zeros_like(sin_ref)


def finish_kernel(t_ref, sq_ref, up_ref, down_ref, cosa_ref, sina_ref, cosb_ref, sinb_ref, sela_ref, selb_ref, o_ref, rot_ref):
    total = sq_ref[...] + get_tail(up_ref) + get_tail(down_ref)
    scale = lax.rsqrt(total / D_WIN + EPSILON)
    eye = identity()
    half = cosa_ref.shape[0]
    out = None
    for row0, cos_ref, sin_ref, sel_ref in ((0, cosa_ref, sina_ref, sela_ref), (half, cosb_ref, sinb_ref, selb_ref)):
        for i in range(half // HEAD):
            at = slice(row0 + i * HEAD, row0 + (i + 1) * HEAD)
            here = slice(i * HEAD, (i + 1) * HEAD)
            r = row0 // HEAD + i
            col = jnp.sum(jnp.where(eye, scale[r : r + 1, :], 0.0), axis=1, keepdims=True)
            v = (t_ref[at, :] + up_ref[at, :].astype(F32) + down_ref[at, :].astype(F32)) * col
            turned = v * cos_ref[here, :] + pltpu.roll(v, HEAD // 2, 1) * sin_ref[here, :]
            rot_ref[at, :] = turned.astype(BF16)
        part = jnp.dot(sel_ref[...], rot_ref[row0 : row0 + half, :], preferred_element_type=F32)
        out = part if out is None else out + part
    o_ref[...] = out.astype(BF16)


def per_device(hidden, norm_gain, kv_weight, owners, offsets):
    tp = lax.axis_size("tp")
    peers = lax.axis_size("dp")
    rows_dev, feats = hidden.shape
    capacity = 2 * rows_dev // peers
    slots = peers * capacity
    share = kv_weight.shape[1] // tp
    half = rows_dev // 2
    depth = tp // 2
    z = lax.axis_index("tp").astype(jnp.int32)
    zs = z.reshape(1)
    bf = functools.partial(jax.ShapeDtypeStruct, dtype=BF16)
    fl = functools.partial(jax.ShapeDtypeStruct, dtype=F32)

    def up(a):
        return lax.ppermute(a, "tp", [(i, (i + 1) % tp) for i in range(tp)])

    def down(a):
        return lax.ppermute(a, "tp", [(i, (i - 1) % tp) for i in range(tp)])

    gain = norm_gain.reshape(1, feats)
    stay = functools.partial(pltpu.with_memory_space_constraint, memory_space=HBM)
    hidden_h, gain_h, weight_h = stay(hidden), stay(gain), stay(kv_weight)
    parts = 4
    message = bf((rows_dev + TAIL, share))
    hi, lo, sq, first_up = call(
        functools.partial(prep_kernel, depth, tp),
        (bf((rows_dev, feats)), bf((rows_dev, feats)), fl((TAIL // 4, HEAD)), message),
        (zs, hidden_h, gain_h, weight_h),
        (SM, HBM, HBM, HBM),
        2,
        "prep",
        limit=PREP_LIMIT,
        scratch=(
            VM((parts, rows_dev // parts, feats), BF16),
            VM((1, feats), F32),
            VM((feats, share), BF16),
            pltpu.SemaphoreType.DMA((parts + 2,)),
        ),
    )
    common = (zs, hi, lo, kv_weight)
    got_up = up(first_up)
    first_down = call(
        functools.partial(first_kernel, depth + 1, tp), message, (*common, sq), (SM,) + (VM,) * 4, 0.6, "first"
    )
    got_down = down(first_down)

    own = owners.reshape(1, rows_dev)
    pos = offsets.reshape(1, rows_dev)
    freq = jnp.asarray(FREQ).reshape(1, HEAD)

    def terms(shifts, extra=None, ins=(), extra_outs=(), us=1.0):
        outs = tuple(fl((rows_dev, share)) for _ in shifts) + tuple(extra_outs)
        return call(
            functools.partial(term_kernel, shifts, tp, extra, len(ins)),
            outs,
            common + tuple(ins),
            (SM,) + (VM,) * (3 + len(ins)),
            us,
            "term",
        )

    heads = share // HEAD
    pieces = {
        3: (functools.partial(select_piece, 0), (own,), (bf((slots, half)),)),
        4: (functools.partial(select_piece, half), (own,), (bf((slots, half)),)),
        5: (functools.partial(table_piece, 0, heads), (pos, freq), (fl((half, HEAD)),) * 2),
        depth + 1: (functools.partial(table_piece, half, heads), (pos, freq), (fl((half, HEAD)),) * 2),
    }
    extras = []

    def add(t, received):
        return call(add_kernel, message, (t, sq, received), (VM,) * 3, 0.2, "add")

    for s in range(2, depth + 1):
        shifts = (depth + 1 - s,) if s == depth else (depth + 1 - s, tp - (depth - s))
        t, *more = terms(shifts, *pieces.get(s, ()))
        got_up = up(add(t, got_up))
        if s < depth:
            got_down = down(add(more.pop(0), got_down))
        extras += more
    mine, *more = terms((0,), *pieces[depth + 1])
    extras += more
    sela, selb, cosa, sina, cosb, sinb = extras
    out = call(
        finish_kernel,
        bf((slots, share)),
        (mine, sq, got_up, got_down, cosa, sina, cosb, sinb, sela, selb),
        (VM,) * 10,
        3,
        "finish",
        scratch=(VM((rows_dev, share), BF16),),
    )
    received = lax.all_to_all(out.reshape(peers, capacity, share), "dp", split_axis=0, concat_axis=0, tiled=True)
    return received.reshape(slots, share).T


def solution(mesh):
    in_specs = (P("dp", "tp"), P("tp"), P("tp", None), P("dp", None), P("dp"))
    return jax.shard_map(per_device, mesh=mesh, in_specs=in_specs, out_specs=P("tp", "dp"), check_vma=False)
```

```python
import functools

import jax
import jax.numpy as jnp
import numpy as np
from jax import lax
from jax.experimental import pallas as pl
from jax.experimental.pallas import tpu as pltpu
from jax.sharding import PartitionSpec as P

D_WIN = 6144
KV_HEADS = 6
HEAD = 128
EPSILON = 1e-05
ROPE_BASE = 500000.0
PREP_LIMIT = 12
TAIL = 32
VM = pltpu.VMEM
SM = pltpu.SMEM
HBM = pltpu.HBM
F32 = jnp.float32
BF16 = jnp.bfloat16
FREQ = np.tile(ROPE_BASE ** (-np.arange(HEAD // 2) * (2.0 / HEAD)), 2).astype(np.float32)


def call(kernel, outs, ins, spaces, us, name, scratch=(), limit=12):
    return pl.pallas_call(
        kernel,
        out_shape=outs,
        in_specs=[pl.BlockSpec(memory_space=s) for s in spaces],
        out_specs=jax.tree.map(lambda _: pl.BlockSpec(memory_space=VM), outs),
        scratch_shapes=list(scratch),
        cost_estimate=pl.CostEstimate(flops=int(us * 5e8), bytes_accessed=int(us * 2e6), transcendentals=0),
        compiler_params=pltpu.CompilerParams(vmem_limit_bytes=limit << 20),
        name=name,
    )(*ins)


def split3(x):
    a = x.astype(BF16).astype(F32)
    b = (x - a).astype(BF16).astype(F32)
    return a, b, x - a - b


def put_tail(o_ref, x):
    pad = jnp.zeros_like(x)
    o_ref[o_ref.shape[0] - TAIL :, :] = jnp.concatenate([*split3(x), pad], axis=0).astype(BF16)


def get_tail(ref):
    t = ref[ref.shape[0] - TAIL :, :].astype(F32)
    n = TAIL // 4
    return t[:n] + t[n : 2 * n] + t[2 * n : 3 * n]


def block_of(w_ref, z, shift, n):
    c = lax.rem(z + shift, n)
    return w_ref[:, pl.ds(pl.multiple_of(c * HEAD, HEAD), HEAD)]


def dot(h, hi, lo):
    return jnp.dot(h, hi, preferred_element_type=F32) + jnp.dot(h, lo, preferred_element_type=F32)


def widen(w, gain):
    x = w.astype(F32) * gain
    hi = x.astype(BF16)
    return hi, (x - hi.astype(F32)).astype(BF16)


def prep_kernel(shift, n, z_ref, h_ref, g_ref, w_ref, gain_ref, sq_ref, o_ref, h_v, g_v, w_v, sems):
    parts = h_v.shape[0]
    rows = h_v.shape[1]
    c = lax.rem(z_ref[0] + shift, n)
    first = [
        pltpu.make_async_copy(g_ref, g_v, sems.at[parts]),
        pltpu.make_async_copy(w_ref.at[:, pl.ds(pl.multiple_of(c * HEAD, HEAD), HEAD)], w_v, sems.at[parts + 1]),
    ]
    copies = [pltpu.make_async_copy(h_ref.at[pl.ds(p * rows, rows), :], h_v.at[p], sems.at[p]) for p in range(parts)]
    for copy in (*first, *copies):
        copy.start()
    eye = identity()
    first[0].wait()
    for i in range(g_v.shape[0]):
        col = jnp.sum(jnp.where(eye, g_v[i : i + 1, :], 0.0), axis=1, keepdims=True)
        gain_ref[i * HEAD : (i + 1) * HEAD, :] = jnp.broadcast_to(col, (HEAD, HEAD))
    first[1].wait()
    hi, lo = widen(w_v[...], gain_ref[...])
    sums = []
    for p in range(parts):
        copies[p].wait()
        o_ref[p * rows : (p + 1) * rows, :] = dot(h_v[p], hi, lo).astype(BF16)
        h = h_v[p].astype(F32)
        col = jnp.sum(h * h, axis=1, keepdims=True)
        for i in range(rows // HEAD):
            sums.append(jnp.sum(jnp.where(eye, col[i * HEAD : (i + 1) * HEAD, :], 0.0), axis=0, keepdims=True))
    sq = jnp.concatenate(sums, axis=0)
    sq_ref[...] = sq
    put_tail(o_ref, sq)


def term_kernel(shifts, n, extra, n_extra, z_ref, h_ref, gain_ref, w_ref, *refs):
    ins, outs = refs[:n_extra], refs[n_extra:]
    pairs = [widen(block_of(w_ref, z_ref[0], shift, n), gain_ref[...]) for shift in shifts]
    hi = jnp.concatenate([p[0] for p in pairs], axis=1)
    lo = jnp.concatenate([p[1] for p in pairs], axis=1)
    rows = h_ref.shape[0] // 2
    for at in (slice(0, rows), slice(rows, 2 * rows)):
        t = dot(h_ref[at, :], hi, lo)
        for i in range(len(shifts)):
            outs[i][at, :] = t[:, i * HEAD : (i + 1) * HEAD]
    if extra is not None:
        extra(z_ref, *ins, *outs[len(shifts) :])


def first_kernel(shift, n, z_ref, h_ref, gain_ref, w_ref, sq_ref, o_ref):
    hi, lo = widen(block_of(w_ref, z_ref[0], shift, n), gain_ref[...])
    rows = h_ref.shape[0] // 2
    for at in (slice(0, rows), slice(rows, 2 * rows)):
        o_ref[at, :] = dot(h_ref[at, :], hi, lo).astype(BF16)
    put_tail(o_ref, sq_ref[...])


def near_kernel(t_ref, sq_ref, in_ref, o_ref, tot_ref):
    rows = t_ref.shape[0]
    o_ref[...] = t_ref[...] + in_ref[:rows, :].astype(F32)
    tot_ref[...] = sq_ref[...] + get_tail(in_ref)


def add_kernel(t_ref, sq_ref, in_ref, o_ref):
    rows = t_ref.shape[0]
    o_ref[:rows, :] = (t_ref[...] + in_ref[:rows, :].astype(F32)).astype(BF16)
    put_tail(o_ref, sq_ref[...] + get_tail(in_ref))


def select_piece(row0, z_ref, own_ref, sel_ref):
    slots, rows = sel_ref.shape
    capacity = TAIL
    peers = slots // capacity
    own = own_ref[...]
    one = jnp.where(lax.broadcasted_iota(jnp.int32, (peers, own.shape[1]), 0) == own, 1.0, 0.0)
    width = 256
    before = jnp.sum(one[:, :row0], axis=1, keepdims=True) if row0 else jnp.zeros((peers, 1), F32)
    upper = jnp.where(
        lax.broadcasted_iota(jnp.int32, (width, width), 0) < lax.broadcasted_iota(jnp.int32, (width, width), 1), 1.0, 0.0
    ).astype(BF16)
    for i in range(rows // width):
        cols = slice(row0 + i * width, row0 + (i + 1) * width)
        e = one[:, cols]
        seen = jnp.dot(e.astype(BF16), upper, preferred_element_type=F32) + before
        rank = jnp.sum(seen * e, axis=0, keepdims=True)
        before = before + jnp.sum(e, axis=1, keepdims=True)
        slot = own[:, cols] * capacity + rank.astype(jnp.int32)
        at = lax.broadcasted_iota(jnp.int32, (slots, width), 0)
        sel_ref[:, i * width : (i + 1) * width] = jnp.where(at == slot, 1.0, 0.0).astype(BF16)


def identity():
    return lax.broadcasted_iota(jnp.int32, (HEAD, HEAD), 0) == lax.broadcasted_iota(jnp.int32, (HEAD, HEAD), 1)


def table_piece(row0, per_device, z_ref, pos_ref, freq_ref, cos_ref, sin_ref):
    rows = cos_ref.shape[0]
    is_key = z_ref[0] * per_device < KV_HEADS

    @pl.when(is_key)
    def _():
        eye = identity()
        sign = jnp.where(lax.broadcasted_iota(jnp.int32, (1, HEAD), 1) < HEAD // 2, -1.0, 1.0)
        for i in range(rows // HEAD):
            pos = pos_ref[:, row0 + i * HEAD : row0 + (i + 1) * HEAD].astype(F32)
            col = jnp.sum(jnp.where(eye, pos, 0.0), axis=1, keepdims=True)
            angle = col * freq_ref[...]
            at = slice(i * HEAD, (i + 1) * HEAD)
            cos_ref[at, :] = jnp.cos(angle)
            sin_ref[at, :] = jnp.sin(angle) * sign

    @pl.when(jnp.logical_not(is_key))
    def _():
        cos_ref[...] = jnp.ones_like(cos_ref)
        sin_ref[...] = jnp.zeros_like(sin_ref)


def finish_kernel(t_ref, sq_ref, up_ref, cosa_ref, sina_ref, cosb_ref, sinb_ref, sela_ref, selb_ref, o_ref, rot_ref):
    total = sq_ref[...] + get_tail(up_ref)
    scale = lax.rsqrt(total / D_WIN + EPSILON)
    eye = identity()
    half = cosa_ref.shape[0]
    out = None
    for row0, cos_ref, sin_ref, sel_ref in ((0, cosa_ref, sina_ref, sela_ref), (half, cosb_ref, sinb_ref, selb_ref)):
        for i in range(half // HEAD):
            at = slice(row0 + i * HEAD, row0 + (i + 1) * HEAD)
            here = slice(i * HEAD, (i + 1) * HEAD)
            r = row0 // HEAD + i
            col = jnp.sum(jnp.where(eye, scale[r : r + 1, :], 0.0), axis=1, keepdims=True)
            v = (t_ref[at, :] + up_ref[at, :].astype(F32)) * col
            turned = v * cos_ref[here, :] + pltpu.roll(v, HEAD // 2, 1) * sin_ref[here, :]
            rot_ref[at, :] = turned.astype(BF16)
        part = jnp.dot(sel_ref[...], rot_ref[row0 : row0 + half, :], preferred_element_type=F32)
        out = part if out is None else out + part
    o_ref[...] = out.astype(BF16)


def per_device(hidden, norm_gain, kv_weight, owners, offsets):
    tp = lax.axis_size("tp")
    peers = lax.axis_size("dp")
    rows_dev, feats = hidden.shape
    capacity = 2 * rows_dev // peers
    slots = peers * capacity
    share = kv_weight.shape[1] // tp
    half = rows_dev // 2
    depth = tp // 2
    z = lax.axis_index("tp").astype(jnp.int32)
    zs = z.reshape(1)
    bf = functools.partial(jax.ShapeDtypeStruct, dtype=BF16)
    fl = functools.partial(jax.ShapeDtypeStruct, dtype=F32)

    def up(a):
        return lax.ppermute(a, "tp", [(i, (i + 1) % tp) for i in range(tp)])

    def down(a):
        return lax.ppermute(a, "tp", [(i, (i - 1) % tp) for i in range(tp)])

    gain = norm_gain.reshape(feats // HEAD, HEAD)
    stay = functools.partial(pltpu.with_memory_space_constraint, memory_space=HBM)
    hidden_h, gain_h, weight_h = stay(hidden), stay(gain), stay(kv_weight)
    parts = 4
    message = bf((rows_dev + TAIL, share))
    spread, sq, first_up = call(
        functools.partial(prep_kernel, depth, tp),
        (fl((feats, HEAD)), fl((TAIL // 4, HEAD)), message),
        (zs, hidden_h, gain_h, weight_h),
        (SM, HBM, HBM, HBM),
        2,
        "prep",
        limit=PREP_LIMIT,
        scratch=(
            VM((parts, rows_dev // parts, feats), BF16),
            VM((feats // HEAD, HEAD), F32),
            VM((feats, share), BF16),
            pltpu.SemaphoreType.DMA((parts + 2,)),
        ),
    )
    common = (zs, hidden, spread, kv_weight)
    got_up = up(first_up)
    first_down = call(
        functools.partial(first_kernel, depth + 1, tp), message, (*common, sq), (SM,) + (VM,) * 4, 0.6, "first"
    )
    got_down = down(first_down)

    own = owners.reshape(1, rows_dev)
    pos = offsets.reshape(1, rows_dev)
    freq = jnp.asarray(FREQ).reshape(1, HEAD)

    def terms(shifts, extra=None, ins=(), extra_outs=(), us=1.0):
        outs = tuple(fl((rows_dev, share)) for _ in shifts) + tuple(extra_outs)
        return call(
            functools.partial(term_kernel, shifts, tp, extra, len(ins)),
            outs,
            common + tuple(ins),
            (SM,) + (VM,) * (3 + len(ins)),
            us,
            "term",
        )

    heads = share // HEAD
    pieces = {
        3: (functools.partial(select_piece, 0), (own,), (bf((slots, half)),)),
        4: (functools.partial(select_piece, half), (own,), (bf((slots, half)),)),
        5: (functools.partial(table_piece, 0, heads), (pos, freq), (fl((half, HEAD)),) * 2),
        depth + 1: (functools.partial(table_piece, half, heads), (pos, freq), (fl((half, HEAD)),) * 2),
    }
    extras = []

    def add(t, received):
        return call(add_kernel, message, (t, sq, received), (VM,) * 3, 0.2, "add")

    for s in range(2, depth + 1):
        shifts = (depth + 1 - s,) if s == depth else (depth + 1 - s, tp - (depth - s))
        t, *more = terms(shifts, *pieces.get(s, ()))
        got_up = up(add(t, got_up))
        if s < depth:
            got_down = down(add(more.pop(0), got_down))
        extras += more
    mine, *more = terms((0,), *pieces[depth + 1])
    extras += more
    sela, selb, cosa, sina, cosb, sinb = extras
    near, near_sq = call(near_kernel, (fl((rows_dev, share)), fl(sq.shape)), (mine, sq, got_down), (VM,) * 3, 0.2, "near")
    out = call(
        finish_kernel,
        bf((slots, share)),
        (near, near_sq, got_up, cosa, sina, cosb, sinb, sela, selb),
        (VM,) * 9,
        3,
        "finish",
        scratch=(VM((rows_dev, share), BF16),),
    )
    received = lax.all_to_all(out.reshape(peers, capacity, share), "dp", split_axis=0, concat_axis=0, tiled=True)
    return received.reshape(slots, share).T


def solution(mesh):
    in_specs = (P("dp", "tp"), P("tp"), P("tp", None), P("dp", None), P("dp"))
    return jax.shard_map(per_device, mesh=mesh, in_specs=in_specs, out_specs=P("tp", "dp"), check_vma=False)
```

```python
import functools

import jax
import jax.numpy as jnp
import numpy as np
from jax import lax
from jax.experimental import pallas as pl
from jax.experimental.pallas import tpu as pltpu
from jax.sharding import PartitionSpec as P

D_WIN = 6144
KV_HEADS = 6
HEAD = 128
EPSILON = 1e-05
ROPE_BASE = 500000.0
PREP_LIMIT = 12
TAIL = 32
VM = pltpu.VMEM
SM = pltpu.SMEM
HBM = pltpu.HBM
F32 = jnp.float32
BF16 = jnp.bfloat16
FREQ = np.tile(ROPE_BASE ** (-np.arange(HEAD // 2) * (2.0 / HEAD)), 2).astype(np.float32)


def call(kernel, outs, ins, spaces, us, name, scratch=(), limit=12):
    return pl.pallas_call(
        kernel,
        out_shape=outs,
        in_specs=[pl.BlockSpec(memory_space=s) for s in spaces],
        out_specs=jax.tree.map(lambda _: pl.BlockSpec(memory_space=VM), outs),
        scratch_shapes=list(scratch),
        cost_estimate=pl.CostEstimate(flops=int(us * 5e8), bytes_accessed=int(us * 2e6), transcendentals=0),
        compiler_params=pltpu.CompilerParams(vmem_limit_bytes=limit << 20),
        name=name,
    )(*ins)


def split3(x):
    a = x.astype(BF16).astype(F32)
    b = (x - a).astype(BF16).astype(F32)
    return a, b, x - a - b


def put_tail(o_ref, x):
    pad = jnp.zeros_like(x)
    o_ref[o_ref.shape[0] - TAIL :, :] = jnp.concatenate([*split3(x), pad], axis=0).astype(BF16)


def get_tail(ref):
    t = ref[ref.shape[0] - TAIL :, :].astype(F32)
    n = TAIL // 4
    return t[:n] + t[n : 2 * n] + t[2 * n : 3 * n]


def block_of(w_ref, z, shift, n):
    c = lax.rem(z + shift, n)
    return w_ref[:, pl.ds(pl.multiple_of(c * HEAD, HEAD), HEAD)]


def dot(h, hi, lo):
    return jnp.dot(h, hi, preferred_element_type=F32) + jnp.dot(h, lo, preferred_element_type=F32)


def widen(w, gain):
    x = w.astype(F32) * gain
    hi = x.astype(BF16)
    return hi, (x - hi.astype(F32)).astype(BF16)


def prep_kernel(shift, n, parts, z_ref, h_ref, g_ref, w_ref, h_v, gain_ref, sq_ref, o_ref, g_v, w_v, sems):
    rows = h_v.shape[0] // parts
    c = lax.rem(z_ref[0] + shift, n)
    first = [
        pltpu.make_async_copy(g_ref, g_v, sems.at[parts]),
        pltpu.make_async_copy(w_ref.at[:, pl.ds(pl.multiple_of(c * HEAD, HEAD), HEAD)], w_v, sems.at[parts + 1]),
    ]
    blocks = [pl.ds(p * rows, rows) for p in range(parts)]
    copies = [pltpu.make_async_copy(h_ref.at[at, :], h_v.at[at, :], sems.at[p]) for p, at in enumerate(blocks)]
    for copy in (*first, *copies):
        copy.start()
    eye = identity()
    first[0].wait()
    for i in range(g_v.shape[0]):
        col = jnp.sum(jnp.where(eye, g_v[i : i + 1, :], 0.0), axis=1, keepdims=True)
        gain_ref[i * HEAD : (i + 1) * HEAD, :] = jnp.broadcast_to(col, (HEAD, HEAD))
    first[1].wait()
    hi, lo = widen(w_v[...], gain_ref[...])
    sums = []
    for p in range(parts):
        copies[p].wait()
        h = h_v[blocks[p], :]
        o_ref[blocks[p], :] = dot(h, hi, lo).astype(BF16)
        h = h.astype(F32)
        col = jnp.sum(h * h, axis=1, keepdims=True)
        for i in range(rows // HEAD):
            sums.append(jnp.sum(jnp.where(eye, col[i * HEAD : (i + 1) * HEAD, :], 0.0), axis=0, keepdims=True))
    sq = jnp.concatenate(sums, axis=0)
    sq_ref[...] = sq
    put_tail(o_ref, sq)


def term_kernel(shifts, n, extra, n_extra, z_ref, h_ref, gain_ref, w_ref, *refs):
    ins, outs = refs[:n_extra], refs[n_extra:]
    pairs = [widen(block_of(w_ref, z_ref[0], shift, n), gain_ref[...]) for shift in shifts]
    hi = jnp.concatenate([p[0] for p in pairs], axis=1)
    lo = jnp.concatenate([p[1] for p in pairs], axis=1)
    rows = h_ref.shape[0] // 2
    for at in (slice(0, rows), slice(rows, 2 * rows)):
        t = dot(h_ref[at, :], hi, lo)
        for i in range(len(shifts)):
            outs[i][at, :] = t[:, i * HEAD : (i + 1) * HEAD]
    if extra is not None:
        extra(z_ref, *ins, *outs[len(shifts) :])


def first_kernel(shift, n, z_ref, h_ref, gain_ref, sq_ref, w_hbm, w_ref, o_ref, sem):
    copy = pltpu.make_async_copy(w_hbm, w_ref, sem.at[0])
    copy.start()
    put_tail(o_ref, sq_ref[...])
    copy.wait()
    hi, lo = widen(block_of(w_ref, z_ref[0], shift, n), gain_ref[...])
    rows = h_ref.shape[0] // 2
    for at in (slice(0, rows), slice(rows, 2 * rows)):
        o_ref[at, :] = dot(h_ref[at, :], hi, lo).astype(BF16)


def near_kernel(t_ref, sq_ref, in_ref, o_ref, tot_ref):
    rows = t_ref.shape[0]
    o_ref[...] = t_ref[...] + in_ref[:rows, :].astype(F32)
    tot_ref[...] = sq_ref[...] + get_tail(in_ref)


def add_kernel(t_ref, sq_ref, in_ref, o_ref):
    rows = t_ref.shape[0]
    o_ref[:rows, :] = (t_ref[...] + in_ref[:rows, :].astype(F32)).astype(BF16)
    put_tail(o_ref, sq_ref[...] + get_tail(in_ref))


def select_piece(row0, z_ref, own_ref, sel_ref, far_ref):
    near_slots, rows = sel_ref.shape
    capacity = TAIL
    peers = 2 * near_slots // capacity
    own = own_ref[...]
    one = jnp.where(lax.broadcasted_iota(jnp.int32, (peers, own.shape[1]), 0) == own, 1.0, 0.0)
    width = 256
    before = jnp.sum(one[:, :row0], axis=1, keepdims=True) if row0 else jnp.zeros((peers, 1), F32)
    upper = jnp.where(
        lax.broadcasted_iota(jnp.int32, (width, width), 0) < lax.broadcasted_iota(jnp.int32, (width, width), 1), 1.0, 0.0
    ).astype(BF16)
    for i in range(rows // width):
        cols = slice(row0 + i * width, row0 + (i + 1) * width)
        e = one[:, cols]
        seen = jnp.dot(e.astype(BF16), upper, preferred_element_type=F32) + before
        rank = jnp.sum(seen * e, axis=0, keepdims=True)
        before = before + jnp.sum(e, axis=1, keepdims=True)
        slot = own[:, cols] * capacity + rank.astype(jnp.int32)
        slot = jnp.where(slot >= near_slots, slot - near_slots, slot)
        at = lax.broadcasted_iota(jnp.int32, (near_slots, width), 0)
        sel_ref[:, i * width : (i + 1) * width] = jnp.where(at == slot, 1.0, 0.0).astype(BF16)
    eye = identity()
    for i in range(rows // HEAD):
        far = jnp.where(own[:, row0 + i * HEAD : row0 + (i + 1) * HEAD] >= peers // 2, 1.0, 0.0)
        col = jnp.sum(jnp.where(eye, far, 0.0), axis=1, keepdims=True)
        far_ref[i * HEAD : (i + 1) * HEAD, :] = jnp.broadcast_to(col, (HEAD, HEAD))


def identity():
    return lax.broadcasted_iota(jnp.int32, (HEAD, HEAD), 0) == lax.broadcasted_iota(jnp.int32, (HEAD, HEAD), 1)


def table_piece(row0, per_device, z_ref, pos_ref, freq_ref, cos_ref, sin_ref):
    rows = cos_ref.shape[0]
    is_key = z_ref[0] * per_device < KV_HEADS

    @pl.when(is_key)
    def _():
        eye = identity()
        sign = jnp.where(lax.broadcasted_iota(jnp.int32, (1, HEAD), 1) < HEAD // 2, -1.0, 1.0)
        for i in range(rows // HEAD):
            pos = pos_ref[:, row0 + i * HEAD : row0 + (i + 1) * HEAD].astype(F32)
            col = jnp.sum(jnp.where(eye, pos, 0.0), axis=1, keepdims=True)
            angle = col * freq_ref[...]
            at = slice(i * HEAD, (i + 1) * HEAD)
            cos_ref[at, :] = jnp.cos(angle)
            sin_ref[at, :] = jnp.sin(angle) * sign

    @pl.when(jnp.logical_not(is_key))
    def _():
        cos_ref[...] = jnp.ones_like(cos_ref)
        sin_ref[...] = jnp.zeros_like(sin_ref)


def finish_kernel(t_ref, sq_ref, up_ref, cosa_ref, sina_ref, cosb_ref, sinb_ref, sela_ref, fara_ref, selb_ref, farb_ref, o_ref, rot_ref):
    total = sq_ref[...] + get_tail(up_ref)
    scale = lax.rsqrt(total / D_WIN + EPSILON)
    eye = identity()
    half = cosa_ref.shape[0]
    near_slots = sela_ref.shape[0]
    out = None
    for row0, cos_ref, sin_ref, sel_ref, far_ref in (
        (0, cosa_ref, sina_ref, sela_ref, fara_ref),
        (half, cosb_ref, sinb_ref, selb_ref, farb_ref),
    ):
        for i in range(half // HEAD):
            at = slice(row0 + i * HEAD, row0 + (i + 1) * HEAD)
            here = slice(i * HEAD, (i + 1) * HEAD)
            r = row0 // HEAD + i
            col = jnp.sum(jnp.where(eye, scale[r : r + 1, :], 0.0), axis=1, keepdims=True)
            v = (t_ref[at, :] + up_ref[at, :].astype(F32)) * col
            turned = v * cos_ref[here, :] + pltpu.roll(v, HEAD // 2, 1) * sin_ref[here, :]
            far = far_ref[here, :]
            rot_ref[at, :HEAD] = (turned * (1.0 - far)).astype(BF16)
            rot_ref[at, HEAD:] = (turned * far).astype(BF16)
        part = jnp.dot(sel_ref[...], rot_ref[row0 : row0 + half, :], preferred_element_type=F32)
        out = part if out is None else out + part
    o_ref[:near_slots, :] = out[:, :HEAD].astype(BF16)
    o_ref[near_slots:, :] = out[:, HEAD:].astype(BF16)


def per_device(hidden, norm_gain, kv_weight, owners, offsets):
    tp = lax.axis_size("tp")
    peers = lax.axis_size("dp")
    rows_dev, feats = hidden.shape
    capacity = 2 * rows_dev // peers
    slots = peers * capacity
    share = kv_weight.shape[1] // tp
    half = rows_dev // 2
    depth = tp // 2
    z = lax.axis_index("tp").astype(jnp.int32)
    zs = z.reshape(1)
    bf = functools.partial(jax.ShapeDtypeStruct, dtype=BF16)
    fl = functools.partial(jax.ShapeDtypeStruct, dtype=F32)

    def up(a):
        return lax.ppermute(a, "tp", [(i, (i + 1) % tp) for i in range(tp)])

    def down(a):
        return lax.ppermute(a, "tp", [(i, (i - 1) % tp) for i in range(tp)])

    gain = norm_gain.reshape(feats // HEAD, HEAD)
    stay = functools.partial(pltpu.with_memory_space_constraint, memory_space=HBM)
    hidden_h, gain_h, weight_h = stay(hidden), stay(gain), stay(kv_weight)
    parts = 4
    message = bf((rows_dev + TAIL, share))
    held, spread, sq, first_up = call(
        functools.partial(prep_kernel, depth, tp, parts),
        (bf((rows_dev, feats)), fl((feats, HEAD)), fl((TAIL // 4, HEAD)), message),
        (zs, hidden_h, gain_h, weight_h),
        (SM, HBM, HBM, HBM),
        2,
        "prep",
        limit=PREP_LIMIT,
        scratch=(
            VM((feats // HEAD, HEAD), F32),
            VM((feats, share), BF16),
            pltpu.SemaphoreType.DMA((parts + 2,)),
        ),
    )
    got_up = up(first_up)
    weight, first_down = call(
        functools.partial(first_kernel, depth + 1, tp),
        (bf(kv_weight.shape), message),
        (zs, held, spread, sq, weight_h),
        (SM, VM, VM, VM, HBM),
        1.5,
        "first",
        scratch=(pltpu.SemaphoreType.DMA((1,)),),
    )
    common = (zs, held, spread, weight)
    got_down = down(first_down)

    own = owners.reshape(1, rows_dev)
    pos = offsets.reshape(1, rows_dev)
    freq = jnp.asarray(FREQ).reshape(1, HEAD)

    def terms(shifts, extra=None, ins=(), extra_outs=(), us=1.0):
        outs = tuple(fl((rows_dev, share)) for _ in shifts) + tuple(extra_outs)
        return call(
            functools.partial(term_kernel, shifts, tp, extra, len(ins)),
            outs,
            common + tuple(ins),
            (SM,) + (VM,) * (3 + len(ins)),
            us,
            "term",
        )

    heads = share // HEAD
    pieces = {
        3: (functools.partial(select_piece, 0), (own,), (bf((slots // 2, half)), fl((half, HEAD)))),
        4: (functools.partial(select_piece, half), (own,), (bf((slots // 2, half)), fl((half, HEAD)))),
        5: (functools.partial(table_piece, 0, heads), (pos, freq), (fl((half, HEAD)),) * 2),
        depth + 1: (functools.partial(table_piece, half, heads), (pos, freq), (fl((half, HEAD)),) * 2),
    }
    extras = []

    def add(t, received):
        return call(add_kernel, message, (t, sq, received), (VM,) * 3, 0.2, "add")

    for s in range(2, depth + 1):
        shifts = (depth + 1 - s,) if s == depth else (depth + 1 - s, tp - (depth - s))
        t, *more = terms(shifts, *pieces.get(s, ()))
        got_up = up(add(t, got_up))
        if s < depth:
            got_down = down(add(more.pop(0), got_down))
        extras += more
    mine, *more = terms((0,), *pieces[depth + 1])
    extras += more
    sela, fara, selb, farb, cosa, sina, cosb, sinb = extras
    near, near_sq = call(near_kernel, (fl((rows_dev, share)), fl(sq.shape)), (mine, sq, got_down), (VM,) * 3, 0.2, "near")
    out = call(
        finish_kernel,
        bf((slots, share)),
        (near, near_sq, got_up, cosa, sina, cosb, sinb, sela, fara, selb, farb),
        (VM,) * 11,
        3,
        "finish",
        scratch=(VM((rows_dev, 2 * share), BF16),),
    )
    received = lax.all_to_all(out.reshape(peers, capacity, share), "dp", split_axis=0, concat_axis=0, tiled=True)
    return received.reshape(slots, share).T


def solution(mesh):
    in_specs = (P("dp", "tp"), P("tp"), P("tp", None), P("dp", None), P("dp"))
    return jax.shard_map(per_device, mesh=mesh, in_specs=in_specs, out_specs=P("tp", "dp"), check_vma=False)
```

```python
import functools

import jax
import jax.numpy as jnp
import numpy as np
from jax import lax
from jax.experimental import pallas as pl
from jax.experimental.pallas import tpu as pltpu
from jax.sharding import PartitionSpec as P

D_WIN = 6144
KV_HEADS = 6
HEAD = 128
EPSILON = 1e-05
ROPE_BASE = 500000.0
PREP_LIMIT = 12
TAIL = 32
VM = pltpu.VMEM
SM = pltpu.SMEM
HBM = pltpu.HBM
F32 = jnp.float32
BF16 = jnp.bfloat16
FREQ = np.tile(ROPE_BASE ** (-np.arange(HEAD // 2) * (2.0 / HEAD)), 2).astype(np.float32)


def call(kernel, outs, ins, spaces, us, name, scratch=(), limit=12):
    return pl.pallas_call(
        kernel,
        out_shape=outs,
        in_specs=[pl.BlockSpec(memory_space=s) for s in spaces],
        out_specs=jax.tree.map(lambda _: pl.BlockSpec(memory_space=VM), outs),
        scratch_shapes=list(scratch),
        cost_estimate=pl.CostEstimate(flops=int(us * 5e8), bytes_accessed=int(us * 2e6), transcendentals=0),
        compiler_params=pltpu.CompilerParams(vmem_limit_bytes=limit << 20),
        name=name,
    )(*ins)


def split3(x):
    a = x.astype(BF16).astype(F32)
    b = (x - a).astype(BF16).astype(F32)
    return a, b, x - a - b


def put_tail(o_ref, x):
    pad = jnp.zeros_like(x)
    o_ref[o_ref.shape[0] - TAIL :, :] = jnp.concatenate([*split3(x), pad], axis=0).astype(BF16)


def get_tail(ref):
    t = ref[ref.shape[0] - TAIL :, :].astype(F32)
    n = TAIL // 4
    return t[:n] + t[n : 2 * n] + t[2 * n : 3 * n]


def block_of(w_ref, z, shift, n):
    c = lax.rem(z + shift, n)
    return w_ref[:, pl.ds(pl.multiple_of(c * HEAD, HEAD), HEAD)]


def dot(h, hi, lo):
    both = jnp.dot(h, jnp.concatenate([hi, lo], axis=1), preferred_element_type=F32)
    return both[:, : hi.shape[1]] + both[:, hi.shape[1] :]


def widen(w, gain):
    x = w.astype(F32) * gain
    hi = x.astype(BF16)
    return hi, (x - hi.astype(F32)).astype(BF16)


def prep_kernel(shift, n, parts, z_ref, h_ref, g_ref, w_ref, h_v, gain_ref, sq_ref, o_ref, g_v, w_v, sems):
    rows = h_v.shape[0] // parts
    c = lax.rem(z_ref[0] + shift, n)
    first = [
        pltpu.make_async_copy(g_ref, g_v, sems.at[parts]),
        pltpu.make_async_copy(w_ref.at[:, pl.ds(pl.multiple_of(c * HEAD, HEAD), HEAD)], w_v, sems.at[parts + 1]),
    ]
    blocks = [pl.ds(p * rows, rows) for p in range(parts)]
    copies = [pltpu.make_async_copy(h_ref.at[at, :], h_v.at[at, :], sems.at[p]) for p, at in enumerate(blocks)]
    for copy in (*first, *copies):
        copy.start()
    eye = identity()
    first[0].wait()
    for i in range(g_v.shape[0]):
        col = jnp.sum(jnp.where(eye, g_v[i : i + 1, :], 0.0), axis=1, keepdims=True)
        gain_ref[i * HEAD : (i + 1) * HEAD, :] = jnp.broadcast_to(col, (HEAD, HEAD))
    first[1].wait()
    hi, lo = widen(w_v[...], gain_ref[...])
    sums = []
    for p in range(parts):
        copies[p].wait()
        h = h_v[blocks[p], :]
        o_ref[blocks[p], :] = dot(h, hi, lo).astype(BF16)
        h = h.astype(F32)
        h = h * h
        h = sum(h[:, j * HEAD : (j + 1) * HEAD] for j in range(h.shape[1] // HEAD))
        for i in range(rows // HEAD):
            sums.append(jnp.sum(h[i * HEAD : (i + 1) * HEAD, :].T, axis=0, keepdims=True))
    sq = jnp.concatenate(sums, axis=0)
    sq_ref[...] = sq
    put_tail(o_ref, sq)


def term_kernel(shifts, n, extra, n_extra, z_ref, h_ref, gain_ref, w_ref, *refs):
    ins, outs = refs[:n_extra], refs[n_extra:]
    pairs = [widen(block_of(w_ref, z_ref[0], shift, n), gain_ref[...]) for shift in shifts]
    hi = jnp.concatenate([p[0] for p in pairs], axis=1)
    lo = jnp.concatenate([p[1] for p in pairs], axis=1)
    rows = h_ref.shape[0] // 2
    for at in (slice(0, rows), slice(rows, 2 * rows)):
        t = dot(h_ref[at, :], hi, lo)
        for i in range(len(shifts)):
            outs[i][at, :] = t[:, i * HEAD : (i + 1) * HEAD]
    if extra is not None:
        extra(z_ref, *ins, *outs[len(shifts) :])


def first_kernel(shift, n, z_ref, h_ref, gain_ref, sq_ref, w_hbm, w_ref, o_ref, sem):
    copy = pltpu.make_async_copy(w_hbm, w_ref, sem.at[0])
    copy.start()
    put_tail(o_ref, sq_ref[...])
    copy.wait()
    hi, lo = widen(block_of(w_ref, z_ref[0], shift, n), gain_ref[...])
    rows = h_ref.shape[0] // 2
    for at in (slice(0, rows), slice(rows, 2 * rows)):
        o_ref[at, :] = dot(h_ref[at, :], hi, lo).astype(BF16)


def near_kernel(t_ref, sq_ref, in_ref, o_ref, tot_ref):
    rows = t_ref.shape[0]
    o_ref[...] = t_ref[...] + in_ref[:rows, :].astype(F32)
    tot_ref[...] = sq_ref[...] + get_tail(in_ref)


def add_kernel(t_ref, sq_ref, in_ref, o_ref):
    rows = t_ref.shape[0]
    o_ref[:rows, :] = (t_ref[...] + in_ref[:rows, :].astype(F32)).astype(BF16)
    put_tail(o_ref, sq_ref[...] + get_tail(in_ref))


def select_piece(row0, z_ref, own_ref, sel_ref, far_ref):
    near_slots, rows = sel_ref.shape
    capacity = TAIL
    peers = 2 * near_slots // capacity
    own = own_ref[...]
    one = jnp.where(lax.broadcasted_iota(jnp.int32, (peers, own.shape[1]), 0) == own, 1.0, 0.0)
    width = 256
    before = jnp.sum(one[:, :row0], axis=1, keepdims=True) if row0 else jnp.zeros((peers, 1), F32)
    upper = jnp.where(
        lax.broadcasted_iota(jnp.int32, (width, width), 0) < lax.broadcasted_iota(jnp.int32, (width, width), 1), 1.0, 0.0
    ).astype(BF16)
    for i in range(rows // width):
        cols = slice(row0 + i * width, row0 + (i + 1) * width)
        e = one[:, cols]
        seen = jnp.dot(e.astype(BF16), upper, preferred_element_type=F32) + before
        rank = jnp.sum(seen * e, axis=0, keepdims=True)
        before = before + jnp.sum(e, axis=1, keepdims=True)
        slot = own[:, cols] * capacity + rank.astype(jnp.int32)
        slot = jnp.where(slot >= near_slots, slot - near_slots, slot)
        at = lax.broadcasted_iota(jnp.int32, (near_slots, width), 0)
        sel_ref[:, i * width : (i + 1) * width] = jnp.where(at == slot, 1.0, 0.0).astype(BF16)
    eye = identity()
    for i in range(rows // HEAD):
        far = jnp.where(own[:, row0 + i * HEAD : row0 + (i + 1) * HEAD] >= peers // 2, 1.0, 0.0)
        col = jnp.sum(jnp.where(eye, far, 0.0), axis=1, keepdims=True)
        far_ref[i * HEAD : (i + 1) * HEAD, :] = jnp.broadcast_to(col, (HEAD, HEAD))


def identity():
    return lax.broadcasted_iota(jnp.int32, (HEAD, HEAD), 0) == lax.broadcasted_iota(jnp.int32, (HEAD, HEAD), 1)


def table_piece(row0, per_device, z_ref, pos_ref, freq_ref, cos_ref, sin_ref):
    rows = cos_ref.shape[0]
    is_key = z_ref[0] * per_device < KV_HEADS

    @pl.when(is_key)
    def _():
        eye = identity()
        sign = jnp.where(lax.broadcasted_iota(jnp.int32, (1, HEAD), 1) < HEAD // 2, -1.0, 1.0)
        for i in range(rows // HEAD):
            pos = pos_ref[:, row0 + i * HEAD : row0 + (i + 1) * HEAD].astype(F32)
            col = jnp.sum(jnp.where(eye, pos, 0.0), axis=1, keepdims=True)
            angle = col * freq_ref[...]
            at = slice(i * HEAD, (i + 1) * HEAD)
            cos_ref[at, :] = jnp.cos(angle)
            sin_ref[at, :] = jnp.sin(angle) * sign

    @pl.when(jnp.logical_not(is_key))
    def _():
        cos_ref[...] = jnp.ones_like(cos_ref)
        sin_ref[...] = jnp.zeros_like(sin_ref)


def finish_kernel(t_ref, sq_ref, up_ref, cosa_ref, sina_ref, cosb_ref, sinb_ref, sela_ref, fara_ref, selb_ref, farb_ref, o_ref, rot_ref):
    total = sq_ref[...] + get_tail(up_ref)
    scale = lax.rsqrt(total / D_WIN + EPSILON)
    eye = identity()
    half = cosa_ref.shape[0]
    near_slots = sela_ref.shape[0]
    out = None
    for row0, cos_ref, sin_ref, sel_ref, far_ref in (
        (0, cosa_ref, sina_ref, sela_ref, fara_ref),
        (half, cosb_ref, sinb_ref, selb_ref, farb_ref),
    ):
        for i in range(half // HEAD):
            at = slice(row0 + i * HEAD, row0 + (i + 1) * HEAD)
            here = slice(i * HEAD, (i + 1) * HEAD)
            r = row0 // HEAD + i
            col = jnp.sum(jnp.where(eye, scale[r : r + 1, :], 0.0), axis=1, keepdims=True)
            v = (t_ref[at, :] + up_ref[at, :].astype(F32)) * col
            turned = v * cos_ref[here, :] + pltpu.roll(v, HEAD // 2, 1) * sin_ref[here, :]
            far = far_ref[here, :]
            rot_ref[at, :HEAD] = (turned * (1.0 - far)).astype(BF16)
            rot_ref[at, HEAD:] = (turned * far).astype(BF16)
        part = jnp.dot(sel_ref[...], rot_ref[row0 : row0 + half, :], preferred_element_type=F32)
        out = part if out is None else out + part
    o_ref[:near_slots, :] = out[:, :HEAD].astype(BF16)
    o_ref[near_slots:, :] = out[:, HEAD:].astype(BF16)


def per_device(hidden, norm_gain, kv_weight, owners, offsets):
    tp = lax.axis_size("tp")
    peers = lax.axis_size("dp")
    rows_dev, feats = hidden.shape
    capacity = 2 * rows_dev // peers
    slots = peers * capacity
    share = kv_weight.shape[1] // tp
    half = rows_dev // 2
    depth = tp // 2
    z = lax.axis_index("tp").astype(jnp.int32)
    zs = z.reshape(1)
    bf = functools.partial(jax.ShapeDtypeStruct, dtype=BF16)
    fl = functools.partial(jax.ShapeDtypeStruct, dtype=F32)

    def up(a):
        return lax.ppermute(a, "tp", [(i, (i + 1) % tp) for i in range(tp)])

    def down(a):
        return lax.ppermute(a, "tp", [(i, (i - 1) % tp) for i in range(tp)])

    gain = norm_gain.reshape(feats // HEAD, HEAD)
    stay = functools.partial(pltpu.with_memory_space_constraint, memory_space=HBM)
    hidden_h, gain_h, weight_h = stay(hidden), stay(gain), stay(kv_weight)
    parts = 2
    message = bf((rows_dev + TAIL, share))
    held, spread, sq, first_up = call(
        functools.partial(prep_kernel, depth, tp, parts),
        (bf((rows_dev, feats)), fl((feats, HEAD)), fl((TAIL // 4, HEAD)), message),
        (zs, hidden_h, gain_h, weight_h),
        (SM, HBM, HBM, HBM),
        2,
        "prep",
        limit=PREP_LIMIT,
        scratch=(
            VM((feats // HEAD, HEAD), F32),
            VM((feats, share), BF16),
            pltpu.SemaphoreType.DMA((parts + 2,)),
        ),
    )
    got_up = up(first_up)
    weight, first_down = call(
        functools.partial(first_kernel, depth + 1, tp),
        (bf(kv_weight.shape), message),
        (zs, held, spread, sq, weight_h),
        (SM, VM, VM, VM, HBM),
        1.5,
        "first",
        scratch=(pltpu.SemaphoreType.DMA((1,)),),
    )
    common = (zs, held, spread, weight)
    got_down = down(first_down)

    own = owners.reshape(1, rows_dev)
    pos = offsets.reshape(1, rows_dev)
    freq = jnp.asarray(FREQ).reshape(1, HEAD)

    def terms(shifts, extra=None, ins=(), extra_outs=(), us=1.0):
        outs = tuple(fl((rows_dev, share)) for _ in shifts) + tuple(extra_outs)
        return call(
            functools.partial(term_kernel, shifts, tp, extra, len(ins)),
            outs,
            common + tuple(ins),
            (SM,) + (VM,) * (3 + len(ins)),
            us,
            "term",
        )

    heads = share // HEAD
    pieces = {
        3: (functools.partial(select_piece, 0), (own,), (bf((slots // 2, half)), fl((half, HEAD)))),
        4: (functools.partial(select_piece, half), (own,), (bf((slots // 2, half)), fl((half, HEAD)))),
        5: (functools.partial(table_piece, 0, heads), (pos, freq), (fl((half, HEAD)),) * 2),
        depth + 1: (functools.partial(table_piece, half, heads), (pos, freq), (fl((half, HEAD)),) * 2),
    }
    extras = []

    def add(t, received):
        return call(add_kernel, message, (t, sq, received), (VM,) * 3, 0.2, "add")

    for s in range(2, depth + 1):
        shifts = (depth + 1 - s,) if s == depth else (depth + 1 - s, tp - (depth - s))
        t, *more = terms(shifts, *pieces.get(s, ()))
        got_up = up(add(t, got_up))
        if s < depth:
            got_down = down(add(more.pop(0), got_down))
        extras += more
    mine, *more = terms((0,), *pieces[depth + 1])
    extras += more
    sela, fara, selb, farb, cosa, sina, cosb, sinb = extras
    near, near_sq = call(near_kernel, (fl((rows_dev, share)), fl(sq.shape)), (mine, sq, got_down), (VM,) * 3, 0.2, "near")
    out = call(
        finish_kernel,
        bf((slots, share)),
        (near, near_sq, got_up, cosa, sina, cosb, sinb, sela, fara, selb, farb),
        (VM,) * 11,
        3,
        "finish",
        scratch=(VM((rows_dev, 2 * share), BF16),),
    )
    received = lax.all_to_all(out.reshape(peers, capacity, share), "dp", split_axis=0, concat_axis=0, tiled=True)
    return received.reshape(slots, share).T


def solution(mesh):
    in_specs = (P("dp", "tp"), P("tp"), P("tp", None), P("dp", None), P("dp"))
    return jax.shard_map(per_device, mesh=mesh, in_specs=in_specs, out_specs=P("tp", "dp"), check_vma=False)
```

```python
import functools

import jax
import jax.numpy as jnp
import numpy as np
from jax import lax
from jax.experimental import pallas as pl
from jax.experimental.pallas import tpu as pltpu
from jax.sharding import PartitionSpec as P

D_WIN = 6144
KV_HEADS = 6
HEAD = 128
EPSILON = 1e-05
ROPE_BASE = 500000.0
PREP_LIMIT = 12
TAIL = 32
VM = pltpu.VMEM
SM = pltpu.SMEM
HBM = pltpu.HBM
F32 = jnp.float32
BF16 = jnp.bfloat16
FREQ = np.tile(ROPE_BASE ** (-np.arange(HEAD // 2) * (2.0 / HEAD)), 2).astype(np.float32)


def call(kernel, outs, ins, spaces, us, name, scratch=(), limit=12):
    return pl.pallas_call(
        kernel,
        out_shape=outs,
        in_specs=[pl.BlockSpec(memory_space=s) for s in spaces],
        out_specs=jax.tree.map(lambda _: pl.BlockSpec(memory_space=VM), outs),
        scratch_shapes=list(scratch),
        cost_estimate=pl.CostEstimate(flops=int(us * 5e8), bytes_accessed=int(us * 2e6), transcendentals=0),
        compiler_params=pltpu.CompilerParams(vmem_limit_bytes=limit << 20),
        name=name,
    )(*ins)


def split3(x):
    a = x.astype(BF16).astype(F32)
    b = (x - a).astype(BF16).astype(F32)
    return a, b, x - a - b


def put_tail(o_ref, x):
    pad = jnp.zeros_like(x)
    o_ref[o_ref.shape[0] - TAIL :, :] = jnp.concatenate([*split3(x), pad], axis=0).astype(BF16)


def get_tail(ref):
    t = ref[ref.shape[0] - TAIL :, :].astype(F32)
    n = TAIL // 4
    return t[:n] + t[n : 2 * n] + t[2 * n : 3 * n]


def block_of(w_ref, z, shift, n):
    c = lax.rem(z + shift, n)
    return w_ref[:, pl.ds(pl.multiple_of(c * HEAD, HEAD), HEAD)]


def dot(h, hi, lo):
    both = jnp.dot(h, jnp.concatenate([hi, lo], axis=1), preferred_element_type=F32)
    return both[:, : hi.shape[1]] + both[:, hi.shape[1] :]


def widen(w, gain):
    x = w.astype(F32) * gain
    hi = x.astype(BF16)
    return hi, (x - hi.astype(F32)).astype(BF16)


def prep_kernel(shift, n, parts, z_ref, h_ref, g_ref, w_ref, h_v, gain_ref, sq_ref, o_ref, g_v, w_v, sems):
    rows = h_v.shape[0] // parts
    c = lax.rem(z_ref[0] + shift, n)
    first = [
        pltpu.make_async_copy(g_ref, g_v, sems.at[parts]),
        pltpu.make_async_copy(w_ref.at[:, pl.ds(pl.multiple_of(c * HEAD, HEAD), HEAD)], w_v, sems.at[parts + 1]),
    ]
    blocks = [pl.ds(p * rows, rows) for p in range(parts)]
    copies = [pltpu.make_async_copy(h_ref.at[at, :], h_v.at[at, :], sems.at[p]) for p, at in enumerate(blocks)]
    for copy in (*first, *copies):
        copy.start()
    eye = identity()
    first[0].wait()
    for i in range(g_v.shape[0]):
        col = jnp.sum(jnp.where(eye, g_v[i : i + 1, :], 0.0), axis=1, keepdims=True)
        gain_ref[i * HEAD : (i + 1) * HEAD, :] = jnp.broadcast_to(col, (HEAD, HEAD))
    first[1].wait()
    hi, lo = widen(w_v[...], gain_ref[...])
    sums = []
    for p in range(parts):
        copies[p].wait()
        h = h_v[blocks[p], :]
        o_ref[blocks[p], :] = dot(h, hi, lo).astype(BF16)
        h = h.astype(F32)
        h = h * h
        h = sum(h[:, j * HEAD : (j + 1) * HEAD] for j in range(h.shape[1] // HEAD))
        for i in range(rows // HEAD):
            sums.append(jnp.sum(h[i * HEAD : (i + 1) * HEAD, :].T, axis=0, keepdims=True))
    sq = jnp.concatenate(sums, axis=0)
    sq_ref[...] = sq
    put_tail(o_ref, sq)


def term_kernel(shifts, n, extra, n_extra, z_ref, h_ref, gain_ref, w_ref, *refs):
    ins, outs = refs[:n_extra], refs[n_extra:]
    pairs = [widen(block_of(w_ref, z_ref[0], shift, n), gain_ref[...]) for shift in shifts]
    hi = jnp.concatenate([p[0] for p in pairs], axis=1)
    lo = jnp.concatenate([p[1] for p in pairs], axis=1)
    rows = h_ref.shape[0] // 2
    for at in (slice(0, rows), slice(rows, 2 * rows)):
        t = dot(h_ref[at, :], hi, lo)
        for i in range(len(shifts)):
            outs[i][at, :] = t[:, i * HEAD : (i + 1) * HEAD]
    if extra is not None:
        extra(z_ref, *ins, *outs[len(shifts) :])


def first_kernel(shift, n, z_ref, h_ref, gain_ref, sq_ref, w_hbm, w_ref, o_ref, sem):
    copy = pltpu.make_async_copy(w_hbm, w_ref, sem.at[0])
    copy.start()
    put_tail(o_ref, sq_ref[...])
    copy.wait()
    hi, lo = widen(block_of(w_ref, z_ref[0], shift, n), gain_ref[...])
    rows = h_ref.shape[0] // 2
    for at in (slice(0, rows), slice(rows, 2 * rows)):
        o_ref[at, :] = dot(h_ref[at, :], hi, lo).astype(BF16)


def near_kernel(t_ref, sq_ref, in_ref, o_ref, tot_ref):
    rows = t_ref.shape[0]
    o_ref[...] = t_ref[...] + in_ref[:rows, :].astype(F32)
    tot_ref[...] = sq_ref[...] + get_tail(in_ref)


def add_kernel(t_ref, sq_ref, in_ref, o_ref):
    rows = t_ref.shape[0]
    o_ref[:rows, :] = (t_ref[...] + in_ref[:rows, :].astype(F32)).astype(BF16)
    put_tail(o_ref, sq_ref[...] + get_tail(in_ref))


def select_piece(row0, z_ref, own_ref, sel_ref, far_ref):
    near_slots, rows = sel_ref.shape
    capacity = TAIL
    peers = 2 * near_slots // capacity
    own = own_ref[...]
    one = jnp.where(lax.broadcasted_iota(jnp.int32, (peers, own.shape[1]), 0) == own, 1.0, 0.0)
    width = 256
    before = jnp.sum(one[:, :row0], axis=1, keepdims=True) if row0 else jnp.zeros((peers, 1), F32)
    upper = jnp.where(
        lax.broadcasted_iota(jnp.int32, (width, width), 0) < lax.broadcasted_iota(jnp.int32, (width, width), 1), 1.0, 0.0
    ).astype(BF16)
    for i in range(rows // width):
        cols = slice(row0 + i * width, row0 + (i + 1) * width)
        e = one[:, cols]
        seen = jnp.dot(e.astype(BF16), upper, preferred_element_type=F32) + before
        rank = jnp.sum(seen * e, axis=0, keepdims=True)
        before = before + jnp.sum(e, axis=1, keepdims=True)
        slot = own[:, cols] * capacity + rank.astype(jnp.int32)
        slot = jnp.where(slot >= near_slots, slot - near_slots, slot)
        at = lax.broadcasted_iota(jnp.int32, (near_slots, width), 0)
        sel_ref[:, i * width : (i + 1) * width] = jnp.where(at == slot, 1.0, 0.0).astype(BF16)
    eye = identity()
    for i in range(rows // HEAD):
        far = jnp.where(own[:, row0 + i * HEAD : row0 + (i + 1) * HEAD] >= peers // 2, 1.0, 0.0)
        col = jnp.sum(jnp.where(eye, far, 0.0), axis=1, keepdims=True)
        far_ref[i * HEAD : (i + 1) * HEAD, :] = jnp.broadcast_to(col, (HEAD, HEAD)).astype(BF16)


def identity():
    return lax.broadcasted_iota(jnp.int32, (HEAD, HEAD), 0) == lax.broadcasted_iota(jnp.int32, (HEAD, HEAD), 1)


def table_piece(row0, per_device, z_ref, pos_ref, freq_ref, cos_ref, sin_ref):
    rows = cos_ref.shape[0]
    is_key = z_ref[0] * per_device < KV_HEADS

    @pl.when(is_key)
    def _():
        eye = identity()
        sign = jnp.where(lax.broadcasted_iota(jnp.int32, (1, HEAD), 1) < HEAD // 2, -1.0, 1.0)
        for i in range(rows // HEAD):
            pos = pos_ref[:, row0 + i * HEAD : row0 + (i + 1) * HEAD].astype(F32)
            col = jnp.sum(jnp.where(eye, pos, 0.0), axis=1, keepdims=True)
            angle = col * freq_ref[...]
            at = slice(i * HEAD, (i + 1) * HEAD)
            cos_ref[at, :] = jnp.cos(angle)
            sin_ref[at, :] = jnp.sin(angle) * sign

    @pl.when(jnp.logical_not(is_key))
    def _():
        cos_ref[...] = jnp.ones_like(cos_ref)
        sin_ref[...] = jnp.zeros_like(sin_ref)


def finish_kernel(t_ref, sq_ref, up_ref, cosa_ref, sina_ref, cosb_ref, sinb_ref, sela_ref, fara_ref, selb_ref, farb_ref, o_ref, rot_ref):
    total = sq_ref[...] + get_tail(up_ref)
    scale = lax.rsqrt(total / D_WIN + EPSILON)
    eye = identity()
    half = cosa_ref.shape[0]
    near_slots = sela_ref.shape[0]
    out = None
    for row0, cos_ref, sin_ref, sel_ref, far_ref in (
        (0, cosa_ref, sina_ref, sela_ref, fara_ref),
        (half, cosb_ref, sinb_ref, selb_ref, farb_ref),
    ):
        for i in range(half // HEAD):
            at = slice(row0 + i * HEAD, row0 + (i + 1) * HEAD)
            here = slice(i * HEAD, (i + 1) * HEAD)
            r = row0 // HEAD + i
            col = jnp.sum(jnp.where(eye, scale[r : r + 1, :], 0.0), axis=1, keepdims=True)
            v = (t_ref[at, :] + up_ref[at, :].astype(F32)) * col
            turned = v * cos_ref[here, :] + pltpu.roll(v, HEAD // 2, 1) * sin_ref[here, :]
            rot = turned.astype(BF16)
            far = rot * far_ref[here, :]
            rot_ref[at, :HEAD] = rot - far
            rot_ref[at, HEAD:] = far
        part = jnp.dot(sel_ref[...], rot_ref[row0 : row0 + half, :], preferred_element_type=F32)
        out = part if out is None else out + part
    o_ref[:near_slots, :] = out[:, :HEAD].astype(BF16)
    o_ref[near_slots:, :] = out[:, HEAD:].astype(BF16)


def per_device(hidden, norm_gain, kv_weight, owners, offsets):
    tp = lax.axis_size("tp")
    peers = lax.axis_size("dp")
    rows_dev, feats = hidden.shape
    capacity = 2 * rows_dev // peers
    slots = peers * capacity
    share = kv_weight.shape[1] // tp
    half = rows_dev // 2
    depth = tp // 2
    z = lax.axis_index("tp").astype(jnp.int32)
    zs = z.reshape(1)
    bf = functools.partial(jax.ShapeDtypeStruct, dtype=BF16)
    fl = functools.partial(jax.ShapeDtypeStruct, dtype=F32)

    def up(a):
        return lax.ppermute(a, "tp", [(i, (i + 1) % tp) for i in range(tp)])

    def down(a):
        return lax.ppermute(a, "tp", [(i, (i - 1) % tp) for i in range(tp)])

    gain = norm_gain.reshape(feats // HEAD, HEAD)
    stay = functools.partial(pltpu.with_memory_space_constraint, memory_space=HBM)
    hidden_h, gain_h, weight_h = stay(hidden), stay(gain), stay(kv_weight)
    parts = 1
    message = bf((rows_dev + TAIL, share))
    held, spread, sq, first_up = call(
        functools.partial(prep_kernel, depth, tp, parts),
        (bf((rows_dev, feats)), fl((feats, HEAD)), fl((TAIL // 4, HEAD)), message),
        (zs, hidden_h, gain_h, weight_h),
        (SM, HBM, HBM, HBM),
        2,
        "prep",
        limit=PREP_LIMIT,
        scratch=(
            VM((feats // HEAD, HEAD), F32),
            VM((feats, share), BF16),
            pltpu.SemaphoreType.DMA((parts + 2,)),
        ),
    )
    got_up = up(first_up)
    weight, first_down = call(
        functools.partial(first_kernel, depth + 1, tp),
        (bf(kv_weight.shape), message),
        (zs, held, spread, sq, weight_h),
        (SM, VM, VM, VM, HBM),
        1.5,
        "first",
        scratch=(pltpu.SemaphoreType.DMA((1,)),),
    )
    common = (zs, held, spread, weight)
    got_down = down(first_down)

    own = owners.reshape(1, rows_dev)
    pos = offsets.reshape(1, rows_dev)
    freq = jnp.asarray(FREQ).reshape(1, HEAD)

    def terms(shifts, extra=None, ins=(), extra_outs=(), us=1.0):
        outs = tuple(fl((rows_dev, share)) for _ in shifts) + tuple(extra_outs)
        return call(
            functools.partial(term_kernel, shifts, tp, extra, len(ins)),
            outs,
            common + tuple(ins),
            (SM,) + (VM,) * (3 + len(ins)),
            us,
            "term",
        )

    heads = share // HEAD
    pieces = {
        3: (functools.partial(select_piece, 0), (own,), (bf((slots // 2, half)), bf((half, HEAD)))),
        4: (functools.partial(select_piece, half), (own,), (bf((slots // 2, half)), bf((half, HEAD)))),
        5: (functools.partial(table_piece, 0, heads), (pos, freq), (fl((half, HEAD)),) * 2),
        depth + 1: (functools.partial(table_piece, half, heads), (pos, freq), (fl((half, HEAD)),) * 2),
    }
    extras = []

    def add(t, received):
        return call(add_kernel, message, (t, sq, received), (VM,) * 3, 0.2, "add")

    for s in range(2, depth + 1):
        shifts = (depth + 1 - s,) if s == depth else (depth + 1 - s, tp - (depth - s))
        t, *more = terms(shifts, *pieces.get(s, ()))
        got_up = up(add(t, got_up))
        if s < depth:
            got_down = down(add(more.pop(0), got_down))
        extras += more
    mine, *more = terms((0,), *pieces[depth + 1])
    extras += more
    sela, fara, selb, farb, cosa, sina, cosb, sinb = extras
    near, near_sq = call(near_kernel, (fl((rows_dev, share)), fl(sq.shape)), (mine, sq, got_down), (VM,) * 3, 0.2, "near")
    out = call(
        finish_kernel,
        bf((slots, share)),
        (near, near_sq, got_up, cosa, sina, cosb, sinb, sela, fara, selb, farb),
        (VM,) * 11,
        3,
        "finish",
        scratch=(VM((rows_dev, 2 * share), BF16),),
    )
    received = lax.all_to_all(out.reshape(peers, capacity, share), "dp", split_axis=0, concat_axis=0, tiled=True)
    return received.reshape(slots, share).T


def solution(mesh):
    in_specs = (P("dp", "tp"), P("tp"), P("tp", None), P("dp", None), P("dp"))
    return jax.shard_map(per_device, mesh=mesh, in_specs=in_specs, out_specs=P("tp", "dp"), check_vma=False)
```

```python
import functools

import jax
import jax.numpy as jnp
import numpy as np
from jax import lax
from jax.experimental import pallas as pl
from jax.experimental.pallas import tpu as pltpu
from jax.sharding import PartitionSpec as P

D_WIN = 6144
KV_HEADS = 6
HEAD = 128
EPSILON = 1e-05
ROPE_BASE = 500000.0
PREP_LIMIT = 12
TAIL = 32
VM = pltpu.VMEM
SM = pltpu.SMEM
HBM = pltpu.HBM
F32 = jnp.float32
BF16 = jnp.bfloat16
FREQ = np.tile(ROPE_BASE ** (-np.arange(HEAD // 2) * (2.0 / HEAD)), 2).astype(np.float32)


def call(kernel, outs, ins, spaces, us, name, scratch=(), limit=12):
    return pl.pallas_call(
        kernel,
        out_shape=outs,
        in_specs=[pl.BlockSpec(memory_space=s) for s in spaces],
        out_specs=jax.tree.map(lambda _: pl.BlockSpec(memory_space=VM), outs),
        scratch_shapes=list(scratch),
        cost_estimate=pl.CostEstimate(flops=int(us * 5e8), bytes_accessed=int(us * 2e6), transcendentals=0),
        compiler_params=pltpu.CompilerParams(vmem_limit_bytes=limit << 20),
        name=name,
    )(*ins)


def split3(x):
    a = x.astype(BF16).astype(F32)
    b = (x - a).astype(BF16).astype(F32)
    return a, b, x - a - b


def put_tail(o_ref, x):
    pad = jnp.zeros_like(x)
    o_ref[o_ref.shape[0] - TAIL :, :] = jnp.concatenate([*split3(x), pad], axis=0).astype(BF16)


def get_tail(ref):
    t = ref[ref.shape[0] - TAIL :, :].astype(F32)
    n = TAIL // 4
    return t[:n] + t[n : 2 * n] + t[2 * n : 3 * n]


def block_of(w_ref, z, shift, n):
    c = lax.rem(z + shift, n)
    return w_ref[:, pl.ds(pl.multiple_of(c * HEAD, HEAD), HEAD)]


def dot(h, hi, lo):
    both = jnp.dot(h, jnp.concatenate([hi, lo], axis=1), preferred_element_type=F32)
    return both[:, : hi.shape[1]] + both[:, hi.shape[1] :]


def widen(w, gain):
    x = w.astype(F32) * gain
    hi = x.astype(BF16)
    return hi, (x - hi.astype(F32)).astype(BF16)


def prep_kernel(shift, n, parts, z_ref, h_ref, g_ref, w_ref, h_v, gain_ref, sq_ref, o_ref, g_v, w_v, sems):
    rows = h_v.shape[0] // parts
    c = lax.rem(z_ref[0] + shift, n)
    first = [
        pltpu.make_async_copy(g_ref, g_v, sems.at[parts]),
        pltpu.make_async_copy(w_ref.at[:, pl.ds(pl.multiple_of(c * HEAD, HEAD), HEAD)], w_v, sems.at[parts + 1]),
    ]
    blocks = [pl.ds(p * rows, rows) for p in range(parts)]
    copies = [pltpu.make_async_copy(h_ref.at[at, :], h_v.at[at, :], sems.at[p]) for p, at in enumerate(blocks)]
    for copy in (*first, *copies):
        copy.start()
    eye = identity()
    first[0].wait()
    for i in range(g_v.shape[0]):
        col = jnp.sum(jnp.where(eye, g_v[i : i + 1, :], 0.0), axis=1, keepdims=True)
        gain_ref[i * HEAD : (i + 1) * HEAD, :] = jnp.broadcast_to(col, (HEAD, HEAD))
    first[1].wait()
    hi, lo = widen(w_v[...], gain_ref[...])
    sums = []
    for p in range(parts):
        copies[p].wait()
        h = h_v[blocks[p], :]
        o_ref[blocks[p], :] = dot(h, hi, lo).astype(BF16)
        h = h.astype(F32)
        h = h * h
        h = sum(h[:, j * HEAD : (j + 1) * HEAD] for j in range(h.shape[1] // HEAD))
        for i in range(rows // HEAD):
            sums.append(jnp.sum(h[i * HEAD : (i + 1) * HEAD, :].T, axis=0, keepdims=True))
    sq = jnp.concatenate(sums, axis=0)
    sq_ref[...] = sq
    put_tail(o_ref, sq)


def term_kernel(shifts, n, extra, n_extra, z_ref, h_ref, gain_ref, w_ref, *refs):
    ins, outs = refs[:n_extra], refs[n_extra:]
    pairs = [widen(block_of(w_ref, z_ref[0], shift, n), gain_ref[...]) for shift in shifts]
    hi = jnp.concatenate([p[0] for p in pairs], axis=1)
    lo = jnp.concatenate([p[1] for p in pairs], axis=1)
    rows = h_ref.shape[0] // 2
    for at in (slice(0, rows), slice(rows, 2 * rows)):
        t = dot(h_ref[at, :], hi, lo)
        for i in range(len(shifts)):
            outs[i][at, :] = t[:, i * HEAD : (i + 1) * HEAD]
    if extra is not None:
        extra(z_ref, *ins, *outs[len(shifts) :])


def first_kernel(shift, n, z_ref, h_ref, gain_ref, sq_ref, w_hbm, w_ref, o_ref, sem):
    copy = pltpu.make_async_copy(w_hbm, w_ref, sem.at[0])
    copy.start()
    put_tail(o_ref, sq_ref[...])
    copy.wait()
    hi, lo = widen(block_of(w_ref, z_ref[0], shift, n), gain_ref[...])
    rows = h_ref.shape[0] // 2
    for at in (slice(0, rows), slice(rows, 2 * rows)):
        o_ref[at, :] = dot(h_ref[at, :], hi, lo).astype(BF16)


def near_kernel(t_ref, sq_ref, in_ref, o_ref, tot_ref):
    rows = t_ref.shape[0]
    o_ref[...] = t_ref[...] + in_ref[:rows, :].astype(F32)
    tot_ref[...] = sq_ref[...] + get_tail(in_ref)


def add_kernel(t_ref, sq_ref, in_ref, o_ref):
    rows = t_ref.shape[0]
    o_ref[:rows, :] = (t_ref[...] + in_ref[:rows, :].astype(F32)).astype(BF16)
    put_tail(o_ref, sq_ref[...] + get_tail(in_ref))


def select_piece(row0, z_ref, own_ref, sel_ref, far_ref):
    near_slots, rows = sel_ref.shape
    capacity = TAIL
    peers = 2 * near_slots // capacity
    own = own_ref[...]
    one = jnp.where(lax.broadcasted_iota(jnp.int32, (peers, own.shape[1]), 0) == own, 1.0, 0.0)
    width = 256
    before = jnp.sum(one[:, :row0], axis=1, keepdims=True) if row0 else jnp.zeros((peers, 1), F32)
    upper = jnp.where(
        lax.broadcasted_iota(jnp.int32, (width, width), 0) < lax.broadcasted_iota(jnp.int32, (width, width), 1), 1.0, 0.0
    ).astype(BF16)
    for i in range(rows // width):
        cols = slice(row0 + i * width, row0 + (i + 1) * width)
        e = one[:, cols]
        seen = jnp.dot(e.astype(BF16), upper, preferred_element_type=F32) + before
        rank = jnp.sum(seen * e, axis=0, keepdims=True)
        before = before + jnp.sum(e, axis=1, keepdims=True)
        slot = own[:, cols] * capacity + rank.astype(jnp.int32)
        slot = jnp.where(slot >= near_slots, slot - near_slots, slot)
        at = lax.broadcasted_iota(jnp.int32, (near_slots, width), 0)
        sel_ref[:, i * width : (i + 1) * width] = jnp.where(at == slot, 1.0, 0.0).astype(BF16)
    eye = identity()
    for i in range(rows // HEAD):
        far = jnp.where(own[:, row0 + i * HEAD : row0 + (i + 1) * HEAD] >= peers // 2, 1.0, 0.0)
        col = jnp.sum(jnp.where(eye, far, 0.0), axis=1, keepdims=True)
        far_ref[i * HEAD : (i + 1) * HEAD, :] = jnp.broadcast_to(col, (HEAD, HEAD))


def identity():
    return lax.broadcasted_iota(jnp.int32, (HEAD, HEAD), 0) == lax.broadcasted_iota(jnp.int32, (HEAD, HEAD), 1)


def table_piece(row0, per_device, z_ref, pos_ref, freq_ref, cos_ref, sin_ref):
    rows = cos_ref.shape[0]
    is_key = z_ref[0] * per_device < KV_HEADS

    @pl.when(is_key)
    def _():
        eye = identity()
        sign = jnp.where(lax.broadcasted_iota(jnp.int32, (1, HEAD), 1) < HEAD // 2, -1.0, 1.0)
        for i in range(rows // HEAD):
            pos = pos_ref[:, row0 + i * HEAD : row0 + (i + 1) * HEAD].astype(F32)
            col = jnp.sum(jnp.where(eye, pos, 0.0), axis=1, keepdims=True)
            angle = col * freq_ref[...]
            at = slice(i * HEAD, (i + 1) * HEAD)
            cos_ref[at, :] = jnp.cos(angle)
            sin_ref[at, :] = jnp.sin(angle) * sign

    @pl.when(jnp.logical_not(is_key))
    def _():
        cos_ref[...] = jnp.ones_like(cos_ref)
        sin_ref[...] = jnp.zeros_like(sin_ref)


def finish_kernel(t_ref, sq_ref, up_ref, cosa_ref, sina_ref, cosb_ref, sinb_ref, sela_ref, fara_ref, selb_ref, farb_ref, o_ref, rot_ref):
    total = sq_ref[...] + get_tail(up_ref)
    scale = lax.rsqrt(total / D_WIN + EPSILON)
    eye = identity()
    half = cosa_ref.shape[0]
    near_slots = sela_ref.shape[0]
    out = None
    for row0, cos_ref, sin_ref, sel_ref, far_ref in (
        (0, cosa_ref, sina_ref, sela_ref, fara_ref),
        (half, cosb_ref, sinb_ref, selb_ref, farb_ref),
    ):
        for i in range(half // HEAD):
            at = slice(row0 + i * HEAD, row0 + (i + 1) * HEAD)
            here = slice(i * HEAD, (i + 1) * HEAD)
            r = row0 // HEAD + i
            col = jnp.sum(jnp.where(eye, scale[r : r + 1, :], 0.0), axis=1, keepdims=True)
            v = (t_ref[at, :] + up_ref[at, :].astype(F32)) * col
            turned = v * cos_ref[here, :] + pltpu.roll(v, HEAD // 2, 1) * sin_ref[here, :]
            far = far_ref[here, :]
            rot_ref[at, :HEAD] = (turned * (1.0 - far)).astype(BF16)
            rot_ref[at, HEAD:] = (turned * far).astype(BF16)
        part = jnp.dot(sel_ref[...], rot_ref[row0 : row0 + half, :], preferred_element_type=F32)
        out = part if out is None else out + part
    o_ref[:near_slots, :] = out[:, :HEAD].astype(BF16)
    o_ref[near_slots:, :] = out[:, HEAD:].astype(BF16)


def turn_kernel(in_ref, o_ref, t_ref, sems):
    pieces = sems.shape[0]
    rows = in_ref.shape[0] // pieces
    copies = []
    for p in range(pieces):
        at = pl.ds(p * rows, rows)
        t_ref[:, at] = in_ref[at, :].T
        copies.append(pltpu.make_async_copy(t_ref.at[:, at], o_ref.at[:, at], sems.at[p]))
        copies[-1].start()
    for copy in copies:
        copy.wait()


def per_device(hidden, norm_gain, kv_weight, owners, offsets):
    tp = lax.axis_size("tp")
    peers = lax.axis_size("dp")
    rows_dev, feats = hidden.shape
    capacity = 2 * rows_dev // peers
    slots = peers * capacity
    share = kv_weight.shape[1] // tp
    half = rows_dev // 2
    depth = tp // 2
    z = lax.axis_index("tp").astype(jnp.int32)
    zs = z.reshape(1)
    bf = functools.partial(jax.ShapeDtypeStruct, dtype=BF16)
    fl = functools.partial(jax.ShapeDtypeStruct, dtype=F32)

    def up(a):
        return lax.ppermute(a, "tp", [(i, (i + 1) % tp) for i in range(tp)])

    def down(a):
        return lax.ppermute(a, "tp", [(i, (i - 1) % tp) for i in range(tp)])

    gain = norm_gain.reshape(feats // HEAD, HEAD)
    stay = functools.partial(pltpu.with_memory_space_constraint, memory_space=HBM)
    hidden_h, gain_h, weight_h = stay(hidden), stay(gain), stay(kv_weight)
    parts = 2
    message = bf((rows_dev + TAIL, share))
    held, spread, sq, first_up = call(
        functools.partial(prep_kernel, depth, tp, parts),
        (bf((rows_dev, feats)), fl((feats, HEAD)), fl((TAIL // 4, HEAD)), message),
        (zs, hidden_h, gain_h, weight_h),
        (SM, HBM, HBM, HBM),
        2,
        "prep",
        limit=PREP_LIMIT,
        scratch=(
            VM((feats // HEAD, HEAD), F32),
            VM((feats, share), BF16),
            pltpu.SemaphoreType.DMA((parts + 2,)),
        ),
    )
    got_up = up(first_up)
    weight, first_down = call(
        functools.partial(first_kernel, depth + 1, tp),
        (bf(kv_weight.shape), message),
        (zs, held, spread, sq, weight_h),
        (SM, VM, VM, VM, HBM),
        1.5,
        "first",
        scratch=(pltpu.SemaphoreType.DMA((1,)),),
    )
    common = (zs, held, spread, weight)
    got_down = down(first_down)

    own = owners.reshape(1, rows_dev)
    pos = offsets.reshape(1, rows_dev)
    freq = jnp.asarray(FREQ).reshape(1, HEAD)

    def terms(shifts, extra=None, ins=(), extra_outs=(), us=1.0):
        outs = tuple(fl((rows_dev, share)) for _ in shifts) + tuple(extra_outs)
        return call(
            functools.partial(term_kernel, shifts, tp, extra, len(ins)),
            outs,
            common + tuple(ins),
            (SM,) + (VM,) * (3 + len(ins)),
            us,
            "term",
        )

    heads = share // HEAD
    pieces = {
        3: (functools.partial(select_piece, 0), (own,), (bf((slots // 2, half)), fl((half, HEAD)))),
        4: (functools.partial(select_piece, half), (own,), (bf((slots // 2, half)), fl((half, HEAD)))),
        5: (functools.partial(table_piece, 0, heads), (pos, freq), (fl((half, HEAD)),) * 2),
        depth + 1: (functools.partial(table_piece, half, heads), (pos, freq), (fl((half, HEAD)),) * 2),
    }
    extras = []

    def add(t, received):
        return call(add_kernel, message, (t, sq, received), (VM,) * 3, 0.2, "add")

    for s in range(2, depth + 1):
        shifts = (depth + 1 - s,) if s == depth else (depth + 1 - s, tp - (depth - s))
        t, *more = terms(shifts, *pieces.get(s, ()))
        got_up = up(add(t, got_up))
        if s < depth:
            got_down = down(add(more.pop(0), got_down))
        extras += more
    mine, *more = terms((0,), *pieces[depth + 1])
    extras += more
    sela, fara, selb, farb, cosa, sina, cosb, sinb = extras
    near, near_sq = call(near_kernel, (fl((rows_dev, share)), fl(sq.shape)), (mine, sq, got_down), (VM,) * 3, 0.2, "near")
    out = call(
        finish_kernel,
        bf((slots, share)),
        (near, near_sq, got_up, cosa, sina, cosb, sinb, sela, fara, selb, farb),
        (VM,) * 11,
        3,
        "finish",
        scratch=(VM((rows_dev, 2 * share), BF16),),
    )
    received = lax.all_to_all(out.reshape(peers, capacity, share), "dp", split_axis=0, concat_axis=0, tiled=True)
    return pl.pallas_call(
        turn_kernel,
        out_shape=bf((share, slots)),
        in_specs=[pl.BlockSpec(memory_space=VM)],
        out_specs=pl.BlockSpec(memory_space=HBM),
        scratch_shapes=[VM((share, slots), BF16), pltpu.SemaphoreType.DMA((4,))],
        compiler_params=pltpu.CompilerParams(vmem_limit_bytes=PREP_LIMIT << 20),
        name="turn",
    )(received.reshape(slots, share))


def solution(mesh):
    in_specs = (P("dp", "tp"), P("tp"), P("tp", None), P("dp", None), P("dp"))
    return jax.shard_map(per_device, mesh=mesh, in_specs=in_specs, out_specs=P("tp", "dp"), check_vma=False)
```
